32 devices in a mesh: gx: 2 (over y), gy: 4 (over x, core), gz: 4 (over z).
Axes of the slice: x: 2, y: 2, z: 4, core: 2. Of those that a mesh axis runs over, the one named last changes fastest.
Arguments:
- leaf_coeffs: float32 [512, 1000], P(('gx', 'gy', 'gz')), may hold values from -6 to 6
- operator_blocks: float32 [2, 7, 4, 3, 400], replicated, may hold values from -0.5 to 0.5
- term_ranks: int32 [2, 7], replicated, may hold values from 2 to 4
- target_device: int32 [64, 7, 1], P(('gx', 'gy', 'gz')), may hold values from 0 to 15; in each aligned block of 14 rows (0 to 13, 14 to 27, ..., all dimensions but the last counted through in order) at most 2 rows name the same one
- target_slot: int32 [64, 7], P(('gx', 'gy', 'gz')), may hold values from 0 to 1
- coarse_targets: int32 [16, 7], P(('gx', 'gy')), may hold values from 0 to 15
- parent_place: int32 [8, 8], P(('gx', 'gy')), may hold values from 0 to 15, as said below
Outputs:
- leaf_result: float32 [512, 1000], P(('gx', 'gy', 'gz'))
The draws below stay inside these ranges and needn't reach their ends.
Inputs may be any that keep to these rules, and one draw needn't show every extreme that they name: `parent_place`: each row names distinct values. `target_device`: among the rows of one device, no value is named more than 2 times.
All inputs are finite; a program needn't handle non-finite values.
Results may differ from the reference program's by a relative error of at most 0.0003.
Values sent between devices are 32-bit elements; how exact they have to be, the bound alone decides.
A program may use at most 64 MiB of HBM per device.

```python
import math
import jax
import jax.numpy as jnp
import numpy as np
from jax import lax

ORDER = 10
TERMS = 4
DISP = 7
NODES1 = 2
C0 = 2
COLUMNS = 8
COLUMN1 = 8
NODES_ALL = 64
LEAVES = 512
NODES0_ALL = 16
CAP1 = 2
N_GY = 4
N_GZ = 4


def draw_parent_place(key, part):
    column_keys = jax.random.split(jax.random.fold_in(key, 17), COLUMNS)

    def one_column(column_key):
        return jax.random.permutation(column_key, C0 * 8)[:COLUMN1]
    return jax.vmap(one_column)(column_keys).astype(jnp.int32)


def touch_ends(array, stream_key, least, largest):
    longest = array.shape.index(max(array.shape))
    spots = []
    for shift in (0, 1):
        where = [jax.random.randint(jax.random.fold_in(stream_key, axis), (), 0, length) for axis, length in enumerate(array.shape)]
        where[longest] = (where[longest] + shift) % array.shape[longest]
        spots.append(tuple(where))
    return array.at[spots[0]].set(least).at[spots[1]].set(largest)


def levels(own_key, dims, pieces, smallest, largest):
    def one(dim, parts):
        heights = jax.random.uniform(jax.random.fold_in(jax.random.fold_in(own_key, 6), dim), (parts,), jnp.float32, smallest / len(pieces), largest / len(pieces))
        return jnp.repeat(jnp.exp(heights), dims[dim] // parts).reshape((-1,) + (1,) * (len(dims) - dim - 1))

    level = one(*pieces[0])
    for cut in pieces[1:]:
        level = level * one(*cut)
    return level


def assign_block(stream_key, own, number, rows, amount, top, reach, skew):
    sequence = jax.random.permutation(stream_key, amount)
    packed, usual = load_shares(amount, rows * top, reach, skew, True), load_shares(amount, rows * top, reach, skew, False)
    places = jnp.arange(amount)

    def named(tallies, turn):
        used = int((tallies > 0).sum())
        fixed = max(1, used // 4)
        shifted = fixed + (places - fixed + turn * (used - fixed)) % max(1, amount - fixed)
        return jnp.zeros((amount,), jnp.int32).at[sequence[jnp.where(places < fixed, places, shifted)]].set(jnp.asarray(tallies, jnp.int32))

    tallies = jnp.where(number % 4 == 0, named(packed, number // 4), named(usual, number - number // 4 - 1))
    mixed = jax.random.permutation(jax.random.fold_in(own, 3), amount)
    giver, taker = mixed[0:amount // 2 * 2:2], mixed[1:amount // 2 * 2:2]
    margin = jnp.minimum(tallies[giver] - 1, reach - tallies[taker]) // 2
    margin = jnp.where((giver == sequence[0]) | (taker == sequence[0]) | (tallies[taker] == 0), 0, jnp.maximum(margin, 0))
    shifted = jax.random.randint(jax.random.fold_in(own, 4), (amount // 2,), 0, 1 << 20) % (margin + 1)
    tallies = tallies.at[giver].add(-shifted).at[taker].add(shifted)
    members = jnp.searchsorted(jnp.cumsum(tallies), jnp.arange(rows * top), side="right").astype(jnp.int32)
    grid = members.reshape(top, rows).T
    grid = grid[jax.random.permutation(jax.random.fold_in(own, 1), rows)]
    turn = jax.random.randint(jax.random.fold_in(own, 2), (rows, 1), 0, top)
    return jnp.take_along_axis(grid, (jnp.arange(top)[None, :] + turn) % top, axis=1)


def load_shares(number_of, total, limit, lean, full):
    weights = [(1 << 20) // math.isqrt(rank ** lean) + 1 for rank in range(1, number_of + 1)]
    largest = limit if full else min(limit, max(-(-total // number_of), total * weights[0] // sum(weights)))
    least = 1 if total - largest >= number_of - 1 else 0
    holding, spare = [largest] + [least] * (number_of - 1), total - largest - least * (number_of - 1)
    while spare > 0:
        movable = [i for i in range(1, number_of) if holding[i] < largest] or [i for i in range(1, number_of) if holding[i] < limit]
        pool, budget = sum([weights[i] for i in movable]), spare
        for i in movable:
            addition = min(limit - holding[i], max(1, budget * weights[i] // pool), spare)
            holding[i] = holding[i] + addition
            spare = spare - addition
    return np.array(holding)


def normal_values(stream_key, dims, width, most, pieces=(), held_as=jnp.bfloat16):
    values = width * jax.random.normal(stream_key, dims, jnp.float32)
    if pieces:
        values = values * levels(stream_key, dims, pieces, -0.22, 0.18)
    return jnp.clip(values, -most, most).astype(held_as)


def setup_inputs(seed: int = 0) -> dict:
    keys = jax.random.split(jax.random.key(seed), 8)
    leaf_coeffs = normal_values(keys[0], (LEAVES, ORDER**3), 1.0, 6.0, ((0, 32),), jnp.float32)
    operator_blocks = normal_values(keys[1], (2, DISP, TERMS, 3, 4 * ORDER**2), (16 * ORDER) ** -0.5, 0.5, (), jnp.float32)
    term_ranks = touch_ends(jax.random.randint(keys[2], (2, DISP), TERMS // 2, TERMS + 1), jax.random.fold_in(keys[2], 1), TERMS // 2, TERMS).astype(jnp.int32)
    target_device_keys = jax.random.split(jax.random.fold_in(keys[3], 1), NODES_ALL * DISP // (NODES1 * DISP))
    target_device_turns = jax.random.permutation(jax.random.fold_in(keys[3], 3), NODES_ALL * DISP // (NODES1 * DISP))
    target_device = jax.vmap(lambda own, number: assign_block(jax.random.fold_in(keys[3], 2), own, number, NODES1 * DISP, N_GY * N_GZ, 1, CAP1, 2))(target_device_keys, target_device_turns).reshape((NODES_ALL, DISP, 1))
    target_slot = touch_ends(jax.random.randint(keys[4], (NODES_ALL, DISP), 0, NODES1), jax.random.fold_in(keys[4], 1), 0, NODES1 - 1).astype(jnp.int32)
    coarse_targets = touch_ends(jax.random.randint(keys[5], (NODES0_ALL, DISP), 0, NODES0_ALL), jax.random.fold_in(keys[5], 1), 0, NODES0_ALL - 1).astype(jnp.int32)
    parent_place = draw_parent_place(jax.random.fold_in(keys[7], 71), 0)
    return {"leaf_coeffs": leaf_coeffs, "operator_blocks": operator_blocks, "term_ranks": term_ranks, "target_device": target_device, "target_slot": target_slot, "coarse_targets": coarse_targets, "parent_place": parent_place}


precise = lax.Precision.HIGHEST

def two_scale(edge_len):
    row_index = jnp.arange(edge_len)[:, None].astype(jnp.float32)
    col_index = jnp.arange(edge_len)[None, :].astype(jnp.float32)
    filter_table = jnp.sqrt(2.0 / edge_len) * jnp.cos(jnp.pi * (col_index + 0.5) * row_index / edge_len)
    return jnp.where(row_index == 0, filter_table * jnp.sqrt(0.5), filter_table)

def transform(blocks, filter_table, inverse):
    if inverse:
        filter_table = filter_table.T
    return jnp.einsum('ix,jy,kz,nxyz->nijk', filter_table, filter_table, filter_table, blocks, precision=precise)

def assemble(leaf_rows, order_len):
    node_count = leaf_rows.shape[0] // 8
    shaped = leaf_rows.reshape(node_count, 2, 2, 2, order_len, order_len, order_len)
    return shaped.transpose(0, 1, 4, 2, 5, 3, 6).reshape(node_count, 2 * order_len, 2 * order_len, 2 * order_len)

def split_octants(blocks, order_len):
    node_count = blocks.shape[0]
    shaped = blocks.reshape(node_count, 2, order_len, 2, order_len, 2, order_len)
    return shaped.transpose(0, 1, 3, 5, 2, 4, 6).reshape(node_count * 8, order_len ** 3)

def displaced(blocks, matrices, rank_now):
    node_count, edge_len = (blocks.shape[0], blocks.shape[1])

    def per_term(running, entries):
        factors, term_index = entries
        flag = (term_index < rank_now).astype(jnp.float32)
        first_factor = factors[0].reshape(edge_len, edge_len) * flag
        second_factor = factors[1].reshape(edge_len, edge_len)
        third_factor = factors[2].reshape(edge_len, edge_len)
        partial_value = jnp.einsum('ia,nabc->nibc', first_factor, blocks, precision=precise)
        partial_value = jnp.einsum('jb,nibc->nijc', second_factor, partial_value, precision=precise)
        partial_value = jnp.einsum('kc,nijc->nijk', third_factor, partial_value, precision=precise)
        return (running + partial_value, None)
    term_index = jnp.arange(matrices.shape[0], dtype=jnp.int32)
    running, _ = lax.scan(per_term, jnp.zeros(blocks.shape, jnp.float32), (matrices, term_index))
    return running.reshape(node_count, edge_len ** 3)

def apply_level(blocks, matrices, ranks, targets, count):

    def per_disp(accumulated, entries):
        matrix_set, rank_now, target = entries
        return (accumulated.at[target].add(displaced(blocks, matrix_set, rank_now)), None)
    start = jnp.zeros((count, blocks.shape[1] ** 3), jnp.float32)
    accumulated, _ = lax.scan(per_disp, start, (matrices, ranks, targets.T))
    return accumulated

def reference(leaf_coeffs, operator_blocks, term_ranks, target_device, target_slot, coarse_targets, parent_place):
    edge_len = 2 * ORDER
    filter_table = two_scale(edge_len)
    node_count = leaf_coeffs.shape[0] // 8
    middle_blocks = transform(assemble(leaf_coeffs, ORDER), filter_table, False)
    corner_parts = middle_blocks[:, :ORDER, :ORDER, :ORDER].reshape(node_count, ORDER ** 3)
    column_count = parent_place.shape[0]
    row_index = (jnp.arange(column_count, dtype=jnp.int32)[:, None] * (8 * C0) + parent_place).reshape(-1).astype(jnp.int32)
    octants = jnp.zeros((column_count * C0 * 8, ORDER ** 3), jnp.float32).at[row_index].set(corner_parts)
    coarse_blocks = transform(assemble(octants, ORDER), filter_table, False)
    coarse_applied = apply_level(coarse_blocks, operator_blocks[0], term_ranks[0], coarse_targets, column_count * C0)
    coarse_back = split_octants(transform(coarse_applied.reshape(-1, edge_len, edge_len, edge_len), filter_table, True), ORDER)
    from_parent = coarse_back[row_index]
    slab_index = jnp.arange(node_count, dtype=jnp.int32) // (NODES1 * N_GY * N_GZ)
    middle_targets = slab_index[:, None] * (N_GY * N_GZ * NODES1) + target_device[:, :, 0] * NODES1 + target_slot
    middle_applied = apply_level(middle_blocks, operator_blocks[1], term_ranks[1], middle_targets.astype(jnp.int32), node_count)
    middle_total = middle_applied.reshape(node_count, edge_len, edge_len, edge_len)
    middle_total = middle_total.at[:, :ORDER, :ORDER, :ORDER].add(from_parent.reshape(node_count, ORDER, ORDER, ORDER))
    return split_octants(transform(middle_total, filter_table, True), ORDER)
```

```python
import functools

import jax
import jax.numpy as jnp
from jax import lax
from jax.experimental import pallas as pl
from jax.experimental.pallas import tpu as pltpu
from jax.sharding import PartitionSpec as P

ORDER = 10
LANES = 128
CHUNK_ROWS = 72

precise = lax.Precision.HIGHEST


def two_scale(edge_len):
    row_index = jnp.arange(edge_len)[:, None].astype(jnp.float32)
    col_index = jnp.arange(edge_len)[None, :].astype(jnp.float32)
    filter_table = jnp.sqrt(2.0 / edge_len) * jnp.cos(
        jnp.pi * (col_index + 0.5) * row_index / edge_len
    )
    return jnp.where(row_index == 0, filter_table * jnp.sqrt(0.5), filter_table)


def transform(blocks, filter_table, inverse):
    if inverse:
        filter_table = filter_table.T
    return jnp.einsum(
        "ix,jy,kz,nxyz->nijk", filter_table, filter_table, filter_table, blocks, precision=precise
    )


def assemble(leaf_rows, order_len):
    node_count = leaf_rows.shape[0] // 8
    shaped = leaf_rows.reshape(node_count, 2, 2, 2, order_len, order_len, order_len)
    return shaped.transpose(0, 1, 4, 2, 5, 3, 6).reshape(
        node_count, 2 * order_len, 2 * order_len, 2 * order_len
    )


def split_octants(blocks, order_len):
    node_count = blocks.shape[0]
    shaped = blocks.reshape(node_count, 2, order_len, 2, order_len, 2, order_len)
    return shaped.transpose(0, 1, 3, 5, 2, 4, 6).reshape(node_count * 8, order_len**3)


def halves(value):
    high = value.astype(jnp.bfloat16)
    low = (value - high.astype(jnp.float32)).astype(jnp.bfloat16)
    return high, low


def nt_dot(a, b):
    return lax.dot_general(a, b, (((1,), (1,)), ((), ())), preferred_element_type=jnp.float32)


def tn_dot(a, b):
    return lax.dot_general(a, b, (((0,), (0,)), ((), ())), preferred_element_type=jnp.float32)


def images_kernel(
    edge, disp, nodes, padded, tiles,
    dest_ref, x_ref, third_ref, second_ref, first_ref, out_ref,
    ping_ref, pong_ref, coef_ref, image_ref,
):
    pairs = first_ref.shape[0]
    width = tiles * LANES
    rows = padded * edge
    spread = (
        lax.broadcasted_iota(jnp.int32, (pairs, width), 1) // edge
        == lax.broadcasted_iota(jnp.int32, (pairs, width), 0)
    ).astype(jnp.bfloat16)

    def fill(slot, source_ref):
        value = source_ref[...]
        high = value.astype(jnp.bfloat16)
        rest = value - high.astype(jnp.float32)
        mid, low = halves(rest)
        table = tn_dot(high, spread) + tn_dot(mid, spread) + tn_dot(low, spread)
        for tile in range(tiles):
            coef_ref[slot, tile] = table[:, tile * LANES:(tile + 1) * LANES]

    fill(0, second_ref)
    fill(1, first_ref)
    x_high, x_low = halves(x_ref[...])
    w_high, w_low = halves(third_ref[...])
    start = nt_dot(x_high, w_high) + (nt_dot(x_high, w_low) + nt_dot(x_low, w_high))
    for tile in range(tiles):
        ping_ref[tile] = start[:, tile * LANES:(tile + 1) * LANES]

    group = 4
    groups = edge // group

    def contract(slot, source_ref, target_ref):
        def step(index, carry):
            tile = index // groups
            first = (index % groups) * group
            sums = [jnp.zeros((rows, LANES), jnp.float32) for _ in range(group)]
            for b in range(edge):
                part = source_ref[tile, pl.ds(b, rows, stride=edge), :]
                for q in range(group):
                    factor = coef_ref[slot, tile, pl.ds((first + q) * edge + b, 1), :]
                    sums[q] = sums[q] + factor * part
            for q in range(group):
                at = pl.multiple_of((first + q) * rows, 8)
                target_ref[tile, pl.ds(at, rows), :] = sums[q]
            return carry

        lax.fori_loop(0, tiles * groups, step, 0)

    contract(0, ping_ref, pong_ref)
    contract(1, pong_ref, ping_ref)

    per_tile = LANES // edge
    columns = 2 * LANES
    lane = lax.broadcasted_iota(jnp.int32, (LANES, columns), 0)
    column = lax.broadcasted_iota(jnp.int32, (LANES, columns), 1)
    column_disp = (column // LANES) * per_tile + (column % LANES) // edge
    column_ok = (column % LANES) < per_tile * edge
    terms = pairs // disp
    total = None
    for tile in range(tiles):
        place = lane + tile * LANES
        pick = (
            (place // (edge * terms) == column_disp) & (place % edge == (column % LANES) % edge)
            & column_ok & (place < pairs * edge)
        ).astype(jnp.bfloat16)
        high, low = halves(ping_ref[tile])
        part = jnp.dot(high, pick, preferred_element_type=jnp.float32) + jnp.dot(
            low, pick, preferred_element_type=jnp.float32
        )
        total = part if total is None else total + part
    used = edge * edge * padded
    for half in range(2):
        image_ref[half, pl.ds(0, used), :] = total[:, half * LANES:(half + 1) * LANES]
        image_ref[half, pl.ds(used, image_ref.shape[1] - used), :] = jnp.zeros(
            (image_ref.shape[1] - used, LANES), jnp.float32
        )
    out_ref[...] = jnp.zeros_like(out_ref)
    out_lane = lax.broadcasted_iota(jnp.int32, (CHUNK_ROWS, LANES), 1) // edge
    for node in range(nodes):
        for e in range(disp):
            packed = jnp.zeros((CHUNK_ROWS, LANES), jnp.float32)
            for q in range(per_tile):
                chunk = image_ref[
                    e // per_tile, pl.ds(q * CHUNK_ROWS * padded + node, CHUNK_ROWS, stride=padded), :
                ]
                shift = (edge * (q - e % per_tile)) % LANES
                if shift:
                    chunk = pltpu.roll(chunk, shift, 1)
                packed = jnp.where(out_lane == q, chunk, packed)
            to = dest_ref[node, e]
            out_ref[to] = out_ref[to] + packed


def images(blocks, matrices, ranks, destination, buffer_rows):
    nodes, edge = blocks.shape[0], blocks.shape[1]
    disp, terms = matrices.shape[0], matrices.shape[1]
    pairs = disp * terms
    padded = nodes + nodes % 2
    tiles = -(-pairs * edge // LANES)
    flat = blocks.reshape(nodes * edge * edge, edge)
    flat = jnp.pad(flat, ((0, (padded - nodes) * edge * edge), (0, 0)))
    keep = (jnp.arange(terms, dtype=jnp.int32)[None, :] < ranks[:, None]).astype(jnp.float32)
    third = (matrices[:, :, 2] * keep[:, :, None]).reshape(pairs * edge, edge)
    third = jnp.pad(third, ((0, tiles * LANES - pairs * edge), (0, 0)))
    second = matrices[:, :, 1].reshape(pairs, edge * edge)
    first = matrices[:, :, 0].reshape(pairs, edge * edge)
    per_tile = LANES // edge
    vmem = pl.BlockSpec(memory_space=pltpu.VMEM)
    return pl.pallas_call(
        functools.partial(images_kernel, edge, disp, nodes, padded, tiles),
        out_shape=jax.ShapeDtypeStruct((buffer_rows, CHUNK_ROWS, LANES), jnp.float32),
        in_specs=[pl.BlockSpec(memory_space=pltpu.SMEM)] + [vmem] * 4,
        out_specs=vmem,
        scratch_shapes=[
            pltpu.VMEM((tiles, padded * edge * edge, LANES), jnp.float32),
            pltpu.VMEM((tiles, padded * edge * edge, LANES), jnp.float32),
            pltpu.VMEM((2, tiles, edge * edge, LANES), jnp.float32),
            pltpu.VMEM((2, padded * CHUNK_ROWS * per_tile, LANES), jnp.float32),
        ],
    )(destination, flat, third, second, first)


def unpack(rows, edge):
    per_tile = LANES // edge
    parts = rows[:, :, :per_tile * edge].reshape(-1, CHUNK_ROWS, per_tile, edge)
    parts = parts.transpose(0, 2, 1, 3).reshape(-1, per_tile * CHUNK_ROWS, edge)
    return parts[:, :edge * edge].reshape(-1, edge, edge, edge)


def on_device(
    leaf_coeffs, operator_blocks, term_ranks, target_device, target_slot, coarse_targets, parent_place
):
    edge_len = 2 * ORDER
    filter_table = two_scale(edge_len)
    node_count = leaf_coeffs.shape[0] // 8
    coarse_count = coarse_targets.shape[0]
    middle_blocks = transform(assemble(leaf_coeffs, ORDER), filter_table, False)
    count_gy = lax.axis_size("gy")
    count_gz = lax.axis_size("gz")
    corner_parts = middle_blocks[:, :ORDER, :ORDER, :ORDER].reshape(1, node_count, ORDER**3)
    column = lax.all_to_all(
        jnp.broadcast_to(corner_parts, (count_gz, node_count, ORDER**3)),
        "gz", split_axis=0, concat_axis=0, tiled=True,
    ).reshape(count_gz * node_count, ORDER**3)
    destination = target_device[:, :, 0] * node_count + target_slot
    middle_buffer = images(
        middle_blocks, operator_blocks[1], term_ranks[1], destination,
        count_gy * count_gz * node_count,
    )
    received = lax.all_to_all(middle_buffer, ("gy", "gz"), split_axis=0, concat_axis=0, tiled=True)
    slot_index = jnp.arange(coarse_count * 8, dtype=jnp.int32)[:, None]
    picker = (slot_index == parent_place[0][None, :]).astype(jnp.float32)
    octants = jnp.dot(picker, column, precision=precise, preferred_element_type=jnp.float32)
    coarse_blocks = transform(assemble(octants, ORDER), filter_table, False)
    buffer_rows = lax.axis_size("gx") * lax.axis_size("gy") * coarse_count
    coarse_buffer = images(
        coarse_blocks, operator_blocks[0], term_ranks[0], coarse_targets, buffer_rows
    )
    arrived = lax.all_to_all(coarse_buffer, ("gx", "gy"), split_axis=0, concat_axis=0, tiled=True)
    coarse_applied = unpack(
        jnp.sum(arrived.reshape(-1, coarse_count, CHUNK_ROWS, LANES), axis=0), edge_len
    )
    coarse_back = split_octants(transform(coarse_applied, filter_table, True), ORDER)
    own_picker = lax.dynamic_slice_in_dim(picker, lax.axis_index("gz") * node_count, node_count, 1)
    from_parent = jnp.dot(
        own_picker.T, coarse_back, precision=precise, preferred_element_type=jnp.float32
    )
    middle_total = unpack(
        jnp.sum(received.reshape(-1, node_count, CHUNK_ROWS, LANES), axis=0), edge_len
    )
    middle_total = middle_total.at[:, :ORDER, :ORDER, :ORDER].add(
        from_parent.reshape(node_count, ORDER, ORDER, ORDER)
    )
    return split_octants(transform(middle_total, filter_table, True), ORDER)


def solution(mesh):
    in_specs = (
        P(("gx", "gy", "gz"), None),
        P(),
        P(),
        P(("gx", "gy", "gz"), None, None),
        P(("gx", "gy", "gz"), None),
        P(("gx", "gy"), None),
        P(("gx", "gy"), None),
    )
    out_specs = P(("gx", "gy", "gz"), None)
    return jax.shard_map(
        on_device, mesh=mesh, in_specs=in_specs, out_specs=out_specs, check_vma=False
    )
```

```python
import functools

import jax
import jax.numpy as jnp
import numpy as np
from jax import lax
from jax.experimental import pallas as pl
from jax.experimental.pallas import tpu as pltpu
from jax.sharding import PartitionSpec as P

ORDER = 10
LANES = 128
CHUNK_ROWS = 72

def ceil_to(value, step):
    return -(-value // step) * step


@functools.cache
def tables(order):
    edge = 2 * order
    i, x = np.arange(edge)[:, None], np.arange(edge)[None, :]
    h = np.sqrt(2.0 / edge) * np.cos(np.pi * (x + 0.5) * i / edge) * np.where(i == 0, np.sqrt(0.5), 1.0)
    face = order * order
    block = ceil_to(face, 8)
    cells = edge * edge
    per_tile = LANES // edge
    square = np.zeros((cells, 4, block))
    whole = np.einsum("ixa,jyb->ijxyab", h.reshape(edge, 2, order), h.reshape(edge, 2, order))
    square[:, :, :face] = whole.reshape(cells, 4, face)
    square = square.reshape(cells, 4 * block)
    low = square.reshape(edge, edge, -1)[:order, :order].reshape(face, -1)
    corner = np.zeros((LANES, 4 * block))
    corner[:face] = low
    forward = np.concatenate([square, corner])
    inverse = np.zeros((4 * block, per_tile * CHUNK_ROWS))
    inverse[:, :cells] = square.T
    inner = np.zeros((4 * block, block))
    inner[:, :face] = low.T
    pad = ceil_to(order, 8)
    lane_place = np.zeros((2, pad, edge))
    lane_back = np.zeros((2, edge, edge))
    for o in range(2):
        lane_place[o, :order] = h.T[o * order:(o + 1) * order]
        lane_back[o, o * order:(o + 1) * order] = h[:order]
    lane_inverse = np.zeros((LANES, edge))
    lane_inverse[:edge] = h
    head = np.zeros((pad, edge))
    head[:] = h[:pad]

    def split(value):
        high = value.astype(np.float32).astype(jnp.bfloat16)
        return np.stack([high, (value - high.astype(np.float64)).astype(np.float32).astype(jnp.bfloat16)])

    plain = lambda value: value.astype(np.float32)
    return dict(
        forward=split(forward), inverse=split(inverse), inner=split(inner),
        h=plain(h), head=plain(head), lane_place=plain(lane_place), lane_back=plain(lane_back),
        lane_inverse=plain(lane_inverse),
    )


def table_dot(table_ref, value, rows=None):
    high, low = halves(value)
    dot = lambda a, b: jnp.dot(a, b, preferred_element_type=jnp.float32)
    first, second = table_ref[0, :rows], table_ref[1, :rows]
    return dot(first, high) + (dot(first, low) + dot(second, high))


def split_dot(dot, a, b):
    a_high, a_low = halves(a)
    b_high, b_low = halves(b)
    return dot(a_high, b_high) + (dot(a_high, b_low) + dot(a_low, b_high))


def nn_dot(a, b):
    return jnp.dot(a, b, preferred_element_type=jnp.float32)


def halves(value):
    high = value.astype(jnp.bfloat16)
    low = (value - high.astype(jnp.float32)).astype(jnp.bfloat16)
    return high, low


def nt_dot(a, b):
    return lax.dot_general(a, b, (((1,), (1,)), ((), ())), preferred_element_type=jnp.float32)


def tn_dot(a, b):
    return lax.dot_general(a, b, (((0,), (0,)), ((), ())), preferred_element_type=jnp.float32)


def images_body(
    edge, disp, nodes, padded, tiles, block_of,
    dest_ref, third_ref, second_ref, first_ref, out_ref,
    ping_ref, pong_ref, coef_ref, image_ref,
):
    pairs = first_ref.shape[0]
    width = tiles * LANES
    rows = padded * edge
    spread = (
        lax.broadcasted_iota(jnp.int32, (pairs, width), 1) // edge
        == lax.broadcasted_iota(jnp.int32, (pairs, width), 0)
    ).astype(jnp.bfloat16)

    def fill(slot, source_ref):
        value = source_ref[...]
        high = value.astype(jnp.bfloat16)
        rest = value - high.astype(jnp.float32)
        mid, low = halves(rest)
        table = tn_dot(high, spread) + tn_dot(mid, spread) + tn_dot(low, spread)
        for tile in range(tiles):
            coef_ref[slot, tile] = table[:, tile * LANES:(tile + 1) * LANES]

    fill(0, second_ref)
    fill(1, first_ref)
    w_high, w_low = halves(third_ref[...])
    cells = edge * edge
    for node in range(padded):
        at = slice(node * cells, (node + 1) * cells)
        if node < nodes:
            x_high, x_low = halves(block_of(node))
            start = nt_dot(x_high, w_high) + (nt_dot(x_high, w_low) + nt_dot(x_low, w_high))
        for tile in range(tiles):
            if node < nodes:
                ping_ref[tile, at, :] = start[:, tile * LANES:(tile + 1) * LANES]
            else:
                ping_ref[tile, at, :] = jnp.zeros((cells, LANES), jnp.float32)

    group = 4
    groups = edge // group

    def contract(slot, source_ref, target_ref):
        def step(index, carry):
            tile = index // groups
            first = (index % groups) * group
            sums = [jnp.zeros((rows, LANES), jnp.float32) for _ in range(group)]
            for b in range(edge):
                part = source_ref[tile, pl.ds(b, rows, stride=edge), :]
                for q in range(group):
                    factor = coef_ref[slot, tile, pl.ds((first + q) * edge + b, 1), :]
                    sums[q] = sums[q] + factor * part
            for q in range(group):
                at = pl.multiple_of((first + q) * rows, 8)
                target_ref[tile, pl.ds(at, rows), :] = sums[q]
            return carry

        lax.fori_loop(0, tiles * groups, step, 0)

    contract(0, ping_ref, pong_ref)
    contract(1, pong_ref, ping_ref)

    per_tile = LANES // edge
    columns = 2 * LANES
    lane = lax.broadcasted_iota(jnp.int32, (LANES, columns), 0)
    column = lax.broadcasted_iota(jnp.int32, (LANES, columns), 1)
    column_disp = (column // LANES) * per_tile + (column % LANES) // edge
    column_ok = (column % LANES) < per_tile * edge
    terms = pairs // disp
    total = None
    for tile in range(tiles):
        place = lane + tile * LANES
        pick = (
            (place // (edge * terms) == column_disp) & (place % edge == (column % LANES) % edge)
            & column_ok & (place < pairs * edge)
        ).astype(jnp.bfloat16)
        high, low = halves(ping_ref[tile])
        part = jnp.dot(high, pick, preferred_element_type=jnp.float32) + jnp.dot(
            low, pick, preferred_element_type=jnp.float32
        )
        total = part if total is None else total + part
    used = edge * edge * padded
    for half in range(2):
        image_ref[half, pl.ds(0, used), :] = total[:, half * LANES:(half + 1) * LANES]
        image_ref[half, pl.ds(used, image_ref.shape[1] - used), :] = jnp.zeros(
            (image_ref.shape[1] - used, LANES), jnp.float32
        )
    out_ref[...] = jnp.zeros_like(out_ref)
    out_lane = lax.broadcasted_iota(jnp.int32, (CHUNK_ROWS, LANES), 1) // edge
    for node in range(nodes):
        for e in range(disp):
            packed = jnp.zeros((CHUNK_ROWS, LANES), jnp.float32)
            for q in range(per_tile):
                chunk = image_ref[
                    e // per_tile, pl.ds(q * CHUNK_ROWS * padded + node, CHUNK_ROWS, stride=padded), :
                ]
                shift = (edge * (q - e % per_tile)) % LANES
                if shift:
                    chunk = pltpu.roll(chunk, shift, 1)
                packed = jnp.where(out_lane == q, chunk, packed)
            to = dest_ref[node, e]
            out_ref[to] = out_ref[to] + packed


def middle_images_kernel(sizes, dest_ref, x_ref, third_ref, second_ref, first_ref, *rest):
    images_body(*sizes, lambda node: x_ref[node], dest_ref, third_ref, second_ref, first_ref, *rest)


def coarse_images_kernel(
    sizes, dest_ref, place_ref, column_ref, square_ref, lane_ref,
    third_ref, second_ref, first_ref, *rest,
):
    members = column_ref.shape[0]
    block = square_ref.shape[2] // 4
    spread = []
    for g in range(members):
        table = jnp.where(place_ref[0, g] % 2 == 0, lane_ref[0], lane_ref[1])
        spread.append(split_dot(tn_dot, column_ref[g], table)[:block])

    def block_of(node):
        parts = []
        for quarter in range(4):
            part = jnp.zeros((block, spread[0].shape[1]), jnp.float32)
            for g in range(members):
                here = place_ref[0, g] // 2 == node * 4 + quarter
                part = part + jnp.where(here, spread[g], 0.0)
            parts.append(part)
        return table_dot(square_ref, jnp.concatenate(parts, axis=0), spread[0].shape[1] ** 2)

    images_body(*sizes, block_of, dest_ref, third_ref, second_ref, first_ref, *rest)


VMEM = pl.BlockSpec(memory_space=pltpu.VMEM)
SMEM = pl.BlockSpec(memory_space=pltpu.SMEM)


def images(kernel, nodes, edge, scalars, extra, matrices, ranks, buffer_rows):
    disp, terms = matrices.shape[0], matrices.shape[1]
    pairs = disp * terms
    padded = nodes + nodes % 2
    tiles = -(-pairs * edge // LANES)
    keep = (jnp.arange(terms, dtype=jnp.int32)[None, :] < ranks[:, None]).astype(jnp.float32)
    third = (matrices[:, :, 2] * keep[:, :, None]).reshape(pairs * edge, edge)
    third = jnp.pad(third, ((0, tiles * LANES - pairs * edge), (0, 0)))
    second = matrices[:, :, 1].reshape(pairs, edge * edge)
    first = matrices[:, :, 0].reshape(pairs, edge * edge)
    per_tile = LANES // edge
    return pl.pallas_call(
        functools.partial(kernel, (edge, disp, nodes, padded, tiles)),
        out_shape=jax.ShapeDtypeStruct((buffer_rows, CHUNK_ROWS, LANES), jnp.float32),
        in_specs=[SMEM] * len(scalars) + [VMEM] * (len(extra) + 3),
        out_specs=VMEM,
        scratch_shapes=[
            pltpu.VMEM((tiles, padded * edge * edge, LANES), jnp.float32),
            pltpu.VMEM((tiles, padded * edge * edge, LANES), jnp.float32),
            pltpu.VMEM((2, tiles, edge * edge, LANES), jnp.float32),
            pltpu.VMEM((2, padded * CHUNK_ROWS * per_tile, LANES), jnp.float32),
        ],
    )(*scalars, *extra, third, second, first)


def forward_kernel(leaf_ref, forward_ref, h_ref, head_ref, x_ref, corner_ref):
    cells = x_ref.shape[1]
    for node in range(x_ref.shape[0]):
        rows = table_dot(forward_ref, leaf_ref[node])
        x_ref[node] = split_dot(nt_dot, rows[:cells], h_ref[...])
        corner_ref[node] = split_dot(nt_dot, head_ref[...], rows[cells:])


def unpacked(packed, edge, scratch_ref):
    for q in range(LANES // edge):
        chunk = pltpu.roll(packed, (LANES - edge * q) % LANES, 1) if q else packed
        scratch_ref[q * CHUNK_ROWS:(q + 1) * CHUNK_ROWS, :] = chunk
    return scratch_ref[...]


def back_kernel(place_ref, arrived_ref, inverse_ref, lane_inverse_ref, lane_back_ref, out_ref, scratch_ref):
    sources, coarse = arrived_ref.shape[:2]
    edge = out_ref.shape[2]
    block = out_ref.shape[1]
    backs = []
    for p in range(coarse):
        total = arrived_ref[0, p]
        for source in range(1, sources):
            total = total + arrived_ref[source, p]
        lanes = split_dot(nn_dot, unpacked(total, edge, scratch_ref), lane_inverse_ref[...])
        backs.append(table_dot(inverse_ref, lanes))
    for node in range(out_ref.shape[0]):
        place = place_ref[0, node]
        part = jnp.zeros((block, edge), jnp.float32)
        for p in range(coarse):
            for quarter in range(4):
                here = place // 2 == p * 4 + quarter
                part = part + jnp.where(here, backs[p][quarter * block:(quarter + 1) * block], 0.0)
        table = jnp.where(place % 2 == 0, lane_back_ref[0], lane_back_ref[1])
        out_ref[node] = split_dot(nn_dot, part, table)


def final_kernel(received_ref, parent_ref, inverse_ref, inner_ref, lane_inverse_ref, out_ref, scratch_ref):
    sources, nodes = received_ref.shape[:2]
    edge = out_ref.shape[2]
    for node in range(nodes):
        total = received_ref[0, node]
        for source in range(1, sources):
            total = total + received_ref[source, node]
        lanes = split_dot(nn_dot, unpacked(total, edge, scratch_ref), lane_inverse_ref[...])
        out_ref[node] = table_dot(inverse_ref, lanes) + table_dot(inner_ref, parent_ref[node])


def on_device(
    leaf_coeffs, operator_blocks, term_ranks, target_device, target_slot, coarse_targets, parent_place
):
    order = ORDER
    edge = 2 * order
    face, cells = order * order, edge * edge
    block = ceil_to(face, 8)
    table = tables(order)
    nodes = leaf_coeffs.shape[0] // 8
    coarse = coarse_targets.shape[0]
    count_gx, count_gy, count_gz = (lax.axis_size(name) for name in ("gx", "gy", "gz"))
    pad = table["head"].shape[0]
    scratch = [pltpu.VMEM((LANES // edge * CHUNK_ROWS, LANES), jnp.float32)]

    leaves = leaf_coeffs.reshape(nodes, 4, 2, face, order).transpose(0, 1, 3, 2, 4)
    leaves = jnp.pad(leaves.reshape(nodes, 4, face, edge), ((0, 0), (0, 0), (0, block - face), (0, 0)))
    middle, corners = pl.pallas_call(
        forward_kernel,
        out_shape=(
            jax.ShapeDtypeStruct((nodes, cells, edge), jnp.float32),
            jax.ShapeDtypeStruct((nodes, pad, LANES), jnp.float32),
        ),
        in_specs=[VMEM] * 4,
        out_specs=(VMEM, VMEM),
    )(leaves.reshape(nodes, 4 * block, edge), table["forward"], table["h"], table["head"])
    column = lax.all_to_all(
        jnp.broadcast_to(corners[None], (count_gz,) + corners.shape).reshape(-1, pad, LANES),
        "gz", split_axis=0, concat_axis=0, tiled=True,
    )
    destination = target_device[:, :, 0] * nodes + target_slot
    middle_buffer = images(
        middle_images_kernel, nodes, edge, (destination,), (middle,),
        operator_blocks[1], term_ranks[1], count_gy * count_gz * nodes,
    )
    middle_buffer, column = lax.optimization_barrier((middle_buffer, column))
    received = lax.all_to_all(middle_buffer, ("gy", "gz"), split_axis=0, concat_axis=0, tiled=True)
    coarse_buffer = images(
        coarse_images_kernel, coarse, edge, (coarse_targets, parent_place),
        (column, table["forward"], table["lane_place"]),
        operator_blocks[0], term_ranks[0], count_gx * count_gy * coarse,
    )
    arrived = lax.all_to_all(coarse_buffer, ("gx", "gy"), split_axis=0, concat_axis=0, tiled=True)
    own_place = lax.dynamic_slice_in_dim(parent_place, lax.axis_index("gz") * nodes, nodes, 1)
    parent = pl.pallas_call(
        back_kernel,
        out_shape=jax.ShapeDtypeStruct((nodes, block, edge), jnp.float32),
        in_specs=[SMEM] + [VMEM] * 4,
        out_specs=VMEM,
        scratch_shapes=scratch,
    )(
        own_place, arrived.reshape(-1, coarse, CHUNK_ROWS, LANES), table["inverse"],
        table["lane_inverse"], table["lane_back"],
    )
    result = pl.pallas_call(
        final_kernel,
        out_shape=jax.ShapeDtypeStruct((nodes, 4 * block, edge), jnp.float32),
        in_specs=[VMEM] * 5,
        out_specs=VMEM,
        scratch_shapes=scratch,
    )(
        received.reshape(-1, nodes, CHUNK_ROWS, LANES), parent, table["inverse"], table["inner"],
        table["lane_inverse"],
    )
    result = result.reshape(nodes, 4, block, 2, order)[:, :, :face]
    return result.transpose(0, 1, 3, 2, 4).reshape(nodes * 8, face * order)


def solution(mesh):
    in_specs = (
        P(("gx", "gy", "gz"), None),
        P(),
        P(),
        P(("gx", "gy", "gz"), None, None),
        P(("gx", "gy", "gz"), None),
        P(("gx", "gy"), None),
        P(("gx", "gy"), None),
    )
    out_specs = P(("gx", "gy", "gz"), None)
    return jax.shard_map(
        on_device, mesh=mesh, in_specs=in_specs, out_specs=out_specs, check_vma=False
    )
```

```python
import functools

import jax
import jax.numpy as jnp
import numpy as np
from jax import lax
from jax.experimental import pallas as pl
from jax.experimental.pallas import tpu as pltpu
from jax.sharding import PartitionSpec as P


ORDER = 10
LANES = 128
CHUNK_ROWS = 72


def ceil_to(value, step):
    return -(-value // step) * step


@functools.cache
def tables(order):
    edge = 2 * order
    i, x = np.arange(edge)[:, None], np.arange(edge)[None, :]
    h = np.sqrt(2.0 / edge) * np.cos(np.pi * (x + 0.5) * i / edge) * np.where(i == 0, np.sqrt(0.5), 1.0)
    face = order * order
    block = ceil_to(face, 8)
    cells = edge * edge
    per_tile = LANES // edge
    square = np.zeros((cells, 4, block))
    whole = np.einsum("ixa,jyb->ijxyab", h.reshape(edge, 2, order), h.reshape(edge, 2, order))
    square[:, :, :face] = whole.reshape(cells, 4, face)
    square = square.reshape(cells, 4 * block)
    low = square.reshape(edge, edge, -1)[:order, :order].reshape(face, -1)
    corner = np.zeros((LANES, 4 * block))
    corner[:face] = low
    forward = np.concatenate([square, corner])
    inverse = np.zeros((4 * block, per_tile * CHUNK_ROWS))
    inverse[:, :cells] = square.T
    inner = np.zeros((4 * block, block))
    inner[:, :face] = low.T
    pad = ceil_to(order, 8)
    lane_place = np.zeros((2, pad, edge))
    lane_back = np.zeros((2, edge, edge))
    for o in range(2):
        lane_place[o, :order] = h.T[o * order:(o + 1) * order]
        lane_back[o, o * order:(o + 1) * order] = h[:order]
    lane_inverse = np.zeros((LANES, edge))
    lane_inverse[:edge] = h
    head = np.zeros((pad, edge))
    head[:] = h[:pad]

    def split(value):
        high = value.astype(np.float32).astype(jnp.bfloat16)
        return np.stack([high, (value - high.astype(np.float64)).astype(np.float32).astype(jnp.bfloat16)])

    plain = lambda value: value.astype(np.float32)
    return dict(
        forward=split(forward), inverse=split(inverse), inner=split(inner),
        h=plain(h), head=plain(head), lane_place=plain(lane_place), lane_back=plain(lane_back),
        lane_inverse=plain(lane_inverse),
    )


def table_dot(table_ref, value, rows=None):
    high, low = halves(value)
    dot = lambda a, b: jnp.dot(a, b, preferred_element_type=jnp.float32)
    first, second = table_ref[0, :rows], table_ref[1, :rows]
    return dot(first, high) + (dot(first, low) + dot(second, high))


def split_dot(dot, a, b):
    a_high, a_low = halves(a)
    b_high, b_low = halves(b)
    return dot(a_high, b_high) + (dot(a_high, b_low) + dot(a_low, b_high))


def nn_dot(a, b):
    return jnp.dot(a, b, preferred_element_type=jnp.float32)


def halves(value):
    high = value.astype(jnp.bfloat16)
    low = (value - high.astype(jnp.float32)).astype(jnp.bfloat16)
    return high, low


def nt_dot(a, b):
    return lax.dot_general(a, b, (((1,), (1,)), ((), ())), preferred_element_type=jnp.float32)


def tn_dot(a, b):
    return lax.dot_general(a, b, (((0,), (0,)), ((), ())), preferred_element_type=jnp.float32)


def images_body(
    edge, disp, nodes, padded, tiles, block_of,
    dest_ref, third_ref, second_ref, first_ref, out_ref,
    ping_ref, pong_ref, coef_ref, image_ref,
):
    pairs = first_ref.shape[0]
    width = tiles * LANES
    rows = padded * edge
    spread = (
        lax.broadcasted_iota(jnp.int32, (pairs, width), 1) // edge
        == lax.broadcasted_iota(jnp.int32, (pairs, width), 0)
    ).astype(jnp.bfloat16)

    def fill(slot, source_ref):
        value = source_ref[...]
        high = value.astype(jnp.bfloat16)
        rest = value - high.astype(jnp.float32)
        mid, low = halves(rest)
        table = tn_dot(high, spread) + tn_dot(mid, spread) + tn_dot(low, spread)
        for tile in range(tiles):
            coef_ref[slot, tile] = table[:, tile * LANES:(tile + 1) * LANES]

    fill(0, second_ref)
    fill(1, first_ref)
    w_high, w_low = halves(third_ref[...])
    cells = edge * edge
    for node in range(padded):
        at = slice(node * cells, (node + 1) * cells)
        if node < nodes:
            x_high, x_low = halves(block_of(node))
            start = nt_dot(x_high, w_high) + (nt_dot(x_high, w_low) + nt_dot(x_low, w_high))
        for tile in range(tiles):
            if node < nodes:
                ping_ref[tile, at, :] = start[:, tile * LANES:(tile + 1) * LANES]
            else:
                ping_ref[tile, at, :] = jnp.zeros((cells, LANES), jnp.float32)

    group = 4
    groups = edge // group

    def contract(slot, source_ref, target_ref):
        def step(index, carry):
            tile = index // groups
            first = (index % groups) * group
            sums = [jnp.zeros((rows, LANES), jnp.float32) for _ in range(group)]
            for b in range(edge):
                part = source_ref[tile, pl.ds(b, rows, stride=edge), :]
                for q in range(group):
                    factor = coef_ref[slot, tile, pl.ds((first + q) * edge + b, 1), :]
                    sums[q] = sums[q] + factor * part
            for q in range(group):
                at = pl.multiple_of((first + q) * rows, 8)
                target_ref[tile, pl.ds(at, rows), :] = sums[q]
            return carry

        lax.fori_loop(0, tiles * groups, step, 0)

    contract(0, ping_ref, pong_ref)
    contract(1, pong_ref, ping_ref)

    per_tile = LANES // edge
    columns = 2 * LANES
    lane = lax.broadcasted_iota(jnp.int32, (LANES, columns), 0)
    column = lax.broadcasted_iota(jnp.int32, (LANES, columns), 1)
    column_disp = (column // LANES) * per_tile + (column % LANES) // edge
    column_ok = (column % LANES) < per_tile * edge
    terms = pairs // disp
    total = None
    for tile in range(tiles):
        place = lane + tile * LANES
        pick = (
            (place // (edge * terms) == column_disp) & (place % edge == (column % LANES) % edge)
            & column_ok & (place < pairs * edge)
        ).astype(jnp.bfloat16)
        high, low = halves(ping_ref[tile])
        part = jnp.dot(high, pick, preferred_element_type=jnp.float32) + jnp.dot(
            low, pick, preferred_element_type=jnp.float32
        )
        total = part if total is None else total + part
    used = edge * edge * padded
    for half in range(2):
        image_ref[half, pl.ds(0, used), :] = total[:, half * LANES:(half + 1) * LANES]
        image_ref[half, pl.ds(used, image_ref.shape[1] - used), :] = jnp.zeros(
            (image_ref.shape[1] - used, LANES), jnp.float32
        )
    out_ref[...] = jnp.zeros_like(out_ref)
    out_lane = lax.broadcasted_iota(jnp.int32, (CHUNK_ROWS, LANES), 1) // edge
    for node in range(nodes):
        for e in range(disp):
            packed = jnp.zeros((CHUNK_ROWS, LANES), jnp.float32)
            for q in range(per_tile):
                chunk = image_ref[
                    e // per_tile, pl.ds(q * CHUNK_ROWS * padded + node, CHUNK_ROWS, stride=padded), :
                ]
                shift = (edge * (q - e % per_tile)) % LANES
                if shift:
                    chunk = pltpu.roll(chunk, shift, 1)
                packed = jnp.where(out_lane == q, chunk, packed)
            to = dest_ref[node, e]
            out_ref[to] = out_ref[to] + packed


def middle_images_kernel(sizes, dest_ref, x_ref, third_ref, second_ref, first_ref, *rest):
    images_body(*sizes, lambda node: x_ref[node], dest_ref, third_ref, second_ref, first_ref, *rest)


def coarse_images_kernel(
    sizes, dest_ref, place_ref, column_ref, square_ref, lane_ref,
    third_ref, second_ref, first_ref, *rest,
):
    members = column_ref.shape[0]
    block = square_ref.shape[2] // 4
    spread = []
    for g in range(members):
        table = jnp.where(place_ref[0, g] % 2 == 0, lane_ref[0], lane_ref[1])
        spread.append(split_dot(tn_dot, column_ref[g], table)[:block])

    def block_of(node):
        parts = []
        for quarter in range(4):
            part = jnp.zeros((block, spread[0].shape[1]), jnp.float32)
            for g in range(members):
                here = place_ref[0, g] // 2 == node * 4 + quarter
                part = part + jnp.where(here, spread[g], 0.0)
            parts.append(part)
        return table_dot(square_ref, jnp.concatenate(parts, axis=0), spread[0].shape[1] ** 2)

    images_body(*sizes, block_of, dest_ref, third_ref, second_ref, first_ref, *rest)


VMEM = pl.BlockSpec(memory_space=pltpu.VMEM)
SMEM = pl.BlockSpec(memory_space=pltpu.SMEM)


def images(kernel, nodes, edge, scalars, extra, matrices, ranks, buffer_rows):
    disp, terms = matrices.shape[0], matrices.shape[1]
    pairs = disp * terms
    padded = nodes + nodes % 2
    tiles = -(-pairs * edge // LANES)
    keep = (jnp.arange(terms, dtype=jnp.int32)[None, :] < ranks[:, None]).astype(jnp.float32)
    third = (matrices[:, :, 2] * keep[:, :, None]).reshape(pairs * edge, edge)
    third = jnp.pad(third, ((0, tiles * LANES - pairs * edge), (0, 0)))
    second = matrices[:, :, 1].reshape(pairs, edge * edge)
    first = matrices[:, :, 0].reshape(pairs, edge * edge)
    per_tile = LANES // edge
    return pl.pallas_call(
        functools.partial(kernel, (edge, disp, nodes, padded, tiles)),
        out_shape=jax.ShapeDtypeStruct((buffer_rows, CHUNK_ROWS, LANES), jnp.float32),
        in_specs=[SMEM] * len(scalars) + [VMEM] * (len(extra) + 3),
        out_specs=VMEM,
        scratch_shapes=[
            pltpu.VMEM((tiles, padded * edge * edge, LANES), jnp.float32),
            pltpu.VMEM((tiles, padded * edge * edge, LANES), jnp.float32),
            pltpu.VMEM((2, tiles, edge * edge, LANES), jnp.float32),
            pltpu.VMEM((2, padded * CHUNK_ROWS * per_tile, LANES), jnp.float32),
        ],
    )(*scalars, *extra, third, second, first)


def group_place(names):
    place, size = 0, 1
    for name in names:
        place = place * lax.axis_size(name) + lax.axis_index(name)
        size = size * lax.axis_size(name)
    return place, size


def group_device(names, place):
    device = {}
    for name in reversed(names):
        device[name] = lax.rem(place, lax.axis_size(name))
        place = place // lax.axis_size(name)
    return device


def greet(names):
    me, size = group_place(names)
    barrier = pltpu.get_barrier_semaphore()
    for step in range(1, size):
        pl.semaphore_signal(
            barrier, inc=1, device_id=group_device(names, lax.rem(me + step, size)),
            device_id_type=pl.DeviceIdType.MESH,
        )
    return lambda: pl.semaphore_wait(barrier, size - 1)


def group_sends(names, source_of, landed_ref, send_sem, recv_sem):
    me, size = group_place(names)
    copies = []
    for step in range(1, size):
        to = lax.rem(me + step, size)
        copies.append(
            pltpu.make_async_remote_copy(
                src_ref=source_of(to), dst_ref=landed_ref.at[me],
                send_sem=send_sem.at[step - 1], recv_sem=recv_sem.at[step - 1],
                device_id=group_device(names, to), device_id_type=pl.DeviceIdType.MESH,
            )
        )
    return copies


def forward_kernel(
    leaf_ref, forward_ref, h_ref, head_ref, x_ref, column_ref, corner_ref, landed_ref, send_sem, recv_sem
):
    names = ("gz",)
    me, size = group_place(names)
    greeted = greet(names)
    cells = x_ref.shape[1]
    nodes = x_ref.shape[0]
    for node in range(nodes):
        rows = table_dot(forward_ref, leaf_ref[node])
        x_ref[node] = split_dot(nt_dot, rows[:cells], h_ref[...])
        corner_ref[node] = split_dot(nt_dot, head_ref[...], rows[cells:])
    greeted()
    copies = group_sends(names, lambda to: corner_ref, landed_ref, send_sem, recv_sem)
    for copy in copies:
        copy.start()
    column_ref[pl.ds(me, 1)] = corner_ref[...][None]
    for step, copy in enumerate(copies, 1):
        copy.wait()
        source = lax.rem(me + size - step, size)
        column_ref[pl.ds(source, 1)] = landed_ref[pl.ds(source, 1)]


def unpacked(packed, edge, scratch_ref):
    for q in range(LANES // edge):
        chunk = pltpu.roll(packed, (LANES - edge * q) % LANES, 1) if q else packed
        scratch_ref[q * CHUNK_ROWS:(q + 1) * CHUNK_ROWS, :] = chunk
    return scratch_ref[...]


def back_kernel(
    place_ref, buffer_ref, inverse_ref, lane_inverse_ref, lane_back_ref, out_ref,
    scratch_ref, landed_ref, send_sem, recv_sem,
):
    names = ("gx", "gy")
    me, size = group_place(names)
    greet(names)()
    copies = group_sends(names, lambda to: buffer_ref.at[to], landed_ref, send_sem, recv_sem)
    for copy in copies:
        copy.start()
    for copy in copies:
        copy.wait()
    coarse = buffer_ref.shape[1]
    edge = out_ref.shape[2]
    block = out_ref.shape[1]
    backs = []
    for p in range(coarse):
        total = buffer_ref[me, p]
        for step in range(1, size):
            total = total + landed_ref[lax.rem(me + size - step, size), p]
        lanes = split_dot(nn_dot, unpacked(total, edge, scratch_ref), lane_inverse_ref[...])
        backs.append(table_dot(inverse_ref, lanes))
    for node in range(out_ref.shape[0]):
        place = place_ref[0, node]
        part = jnp.zeros((block, edge), jnp.float32)
        for p in range(coarse):
            for quarter in range(4):
                here = place // 2 == p * 4 + quarter
                part = part + jnp.where(here, backs[p][quarter * block:(quarter + 1) * block], 0.0)
        table = jnp.where(place % 2 == 0, lane_back_ref[0], lane_back_ref[1])
        out_ref[node] = split_dot(nn_dot, part, table)


def final_kernel(received_ref, parent_ref, inverse_ref, inner_ref, lane_inverse_ref, out_ref, scratch_ref):
    sources, nodes = received_ref.shape[:2]
    edge = out_ref.shape[2]
    for node in range(nodes):
        total = received_ref[0, node]
        for source in range(1, sources):
            total = total + received_ref[source, node]
        lanes = split_dot(nn_dot, unpacked(total, edge, scratch_ref), lane_inverse_ref[...])
        out_ref[node] = table_dot(inverse_ref, lanes) + table_dot(inner_ref, parent_ref[node])


def on_device(
    leaf_coeffs, operator_blocks, term_ranks, target_device, target_slot, coarse_targets, parent_place
):
    order = ORDER
    edge = 2 * order
    face, cells = order * order, edge * edge
    block = ceil_to(face, 8)
    table = tables(order)
    nodes = leaf_coeffs.shape[0] // 8
    coarse = coarse_targets.shape[0]
    count_gx, count_gy, count_gz = (lax.axis_size(name) for name in ("gx", "gy", "gz"))
    pad = table["head"].shape[0]
    scratch = [pltpu.VMEM((LANES // edge * CHUNK_ROWS, LANES), jnp.float32)]

    leaves = leaf_coeffs.reshape(nodes, 4, 2, face, order).transpose(0, 1, 3, 2, 4)
    leaves = jnp.pad(leaves.reshape(nodes, 4, face, edge), ((0, 0), (0, 0), (0, block - face), (0, 0)))
    middle, column = pl.pallas_call(
        forward_kernel,
        out_shape=(
            jax.ShapeDtypeStruct((nodes, cells, edge), jnp.float32),
            jax.ShapeDtypeStruct((count_gz, nodes, pad, LANES), jnp.float32),
        ),
        in_specs=[VMEM] * 4,
        out_specs=(VMEM, VMEM),
        scratch_shapes=[
            pltpu.VMEM((nodes, pad, LANES), jnp.float32),
            pltpu.VMEM((count_gz, nodes, pad, LANES), jnp.float32),
            pltpu.SemaphoreType.DMA((count_gz,)),
            pltpu.SemaphoreType.DMA((count_gz,)),
        ],
        compiler_params=pltpu.CompilerParams(collective_id=0, has_side_effects=True),
    )(leaves.reshape(nodes, 4 * block, edge), table["forward"], table["h"], table["head"])
    column = column.reshape(-1, pad, LANES)
    destination = target_device[:, :, 0] * nodes + target_slot
    middle_buffer = images(
        middle_images_kernel, nodes, edge, (destination,), (middle,),
        operator_blocks[1], term_ranks[1], count_gy * count_gz * nodes,
    )
    middle_buffer, column = lax.optimization_barrier((middle_buffer, column))
    received = lax.all_to_all(middle_buffer, ("gy", "gz"), split_axis=0, concat_axis=0, tiled=True)
    coarse_buffer = images(
        coarse_images_kernel, coarse, edge, (coarse_targets, parent_place),
        (column, table["forward"], table["lane_place"]),
        operator_blocks[0], term_ranks[0], count_gx * count_gy * coarse,
    )
    own_place = lax.dynamic_slice_in_dim(parent_place, lax.axis_index("gz") * nodes, nodes, 1)
    plane = count_gx * count_gy
    parent = pl.pallas_call(
        back_kernel,
        out_shape=jax.ShapeDtypeStruct((nodes, block, edge), jnp.float32),
        in_specs=[SMEM] + [VMEM] * 4,
        out_specs=VMEM,
        scratch_shapes=scratch + [
            pltpu.VMEM((plane, coarse, CHUNK_ROWS, LANES), jnp.float32),
            pltpu.SemaphoreType.DMA((plane,)),
            pltpu.SemaphoreType.DMA((plane,)),
        ],
        compiler_params=pltpu.CompilerParams(collective_id=1, has_side_effects=True),
    )(
        own_place, coarse_buffer.reshape(plane, coarse, CHUNK_ROWS, LANES), table["inverse"],
        table["lane_inverse"], table["lane_back"],
    )
    result = pl.pallas_call(
        final_kernel,
        out_shape=jax.ShapeDtypeStruct((nodes, 4 * block, edge), jnp.float32),
        in_specs=[VMEM] * 5,
        out_specs=VMEM,
        scratch_shapes=scratch,
    )(
        received.reshape(-1, nodes, CHUNK_ROWS, LANES), parent, table["inverse"], table["inner"],
        table["lane_inverse"],
    )
    result = result.reshape(nodes, 4, block, 2, order)[:, :, :face]
    return result.transpose(0, 1, 3, 2, 4).reshape(nodes * 8, face * order)


def solution(mesh):
    in_specs = (
        P(("gx", "gy", "gz"), None),
        P(),
        P(),
        P(("gx", "gy", "gz"), None, None),
        P(("gx", "gy", "gz"), None),
        P(("gx", "gy"), None),
        P(("gx", "gy"), None),
    )
    out_specs = P(("gx", "gy", "gz"), None)
    return jax.shard_map(
        on_device, mesh=mesh, in_specs=in_specs, out_specs=out_specs, check_vma=False
    )
```

```python
import functools

import jax
import jax.numpy as jnp
import numpy as np
from jax import lax
from jax.experimental import pallas as pl
from jax.experimental.pallas import tpu as pltpu
from jax.sharding import PartitionSpec as P


ORDER = 10
LANES = 128
CHUNK_ROWS = 72


def ceil_to(value, step):
    return -(-value // step) * step


@functools.cache
def tables(order):
    edge = 2 * order
    i, x = np.arange(edge)[:, None], np.arange(edge)[None, :]
    h = np.sqrt(2.0 / edge) * np.cos(np.pi * (x + 0.5) * i / edge) * np.where(i == 0, np.sqrt(0.5), 1.0)
    face = order * order
    block = ceil_to(face, 8)
    cells = edge * edge
    per_tile = LANES // edge
    square = np.zeros((cells, 4, block))
    whole = np.einsum("ixa,jyb->ijxyab", h.reshape(edge, 2, order), h.reshape(edge, 2, order))
    square[:, :, :face] = whole.reshape(cells, 4, face)
    square = square.reshape(cells, 4 * block)
    low = square.reshape(edge, edge, -1)[:order, :order].reshape(face, -1)
    corner = np.zeros((LANES, 4 * block))
    corner[:face] = low
    forward = np.concatenate([square, corner])
    inverse = np.zeros((4 * block, per_tile * CHUNK_ROWS))
    inverse[:, :cells] = square.T
    inner = np.zeros((4 * block, block))
    inner[:, :face] = low.T
    pad = ceil_to(order, 8)
    lane_place = np.zeros((2, pad, edge))
    lane_back = np.zeros((2, edge, edge))
    for o in range(2):
        lane_place[o, :order] = h.T[o * order:(o + 1) * order]
        lane_back[o, o * order:(o + 1) * order] = h[:order]
    lane_inverse = np.zeros((LANES, edge))
    lane_inverse[:edge] = h
    head = np.zeros((pad, edge))
    head[:] = h[:pad]

    def split(value):
        high = value.astype(np.float32).astype(jnp.bfloat16)
        return np.stack([high, (value - high.astype(np.float64)).astype(np.float32).astype(jnp.bfloat16)])

    plain = lambda value: value.astype(np.float32)
    return dict(
        forward=split(forward), inverse=split(inverse), inner=split(inner),
        h=plain(h), head=plain(head), lane_place=plain(lane_place), lane_back=plain(lane_back),
        lane_inverse=plain(lane_inverse),
    )


def table_dot(table_ref, value, rows=None):
    high, low = halves(value)
    dot = lambda a, b: jnp.dot(a, b, preferred_element_type=jnp.float32)
    first, second = table_ref[0, :rows], table_ref[1, :rows]
    return dot(first, high) + (dot(first, low) + dot(second, high))


def split_dot(dot, a, b):
    a_high, a_low = halves(a)
    b_high, b_low = halves(b)
    return dot(a_high, b_high) + (dot(a_high, b_low) + dot(a_low, b_high))


def nn_dot(a, b):
    return jnp.dot(a, b, preferred_element_type=jnp.float32)


def halves(value):
    high = value.astype(jnp.bfloat16)
    low = (value - high.astype(jnp.float32)).astype(jnp.bfloat16)
    return high, low


def nt_dot(a, b):
    return lax.dot_general(a, b, (((1,), (1,)), ((), ())), preferred_element_type=jnp.float32)


def tn_dot(a, b):
    return lax.dot_general(a, b, (((0,), (0,)), ((), ())), preferred_element_type=jnp.float32)


def images_body(
    edge, disp, nodes, padded, tiles, block_of,
    level, dest_ref, third_ref, factors_ref, out_ref,
    ping_ref, pong_ref, coef_ref, image_ref,
):
    pairs = factors_ref.shape[2]
    width = tiles * LANES
    rows = padded * edge
    spread = (
        lax.broadcasted_iota(jnp.int32, (pairs, width), 1) // edge
        == lax.broadcasted_iota(jnp.int32, (pairs, width), 0)
    ).astype(jnp.bfloat16)

    def fill(slot, value):
        high = value.astype(jnp.bfloat16)
        rest = value - high.astype(jnp.float32)
        mid, low = halves(rest)
        table = tn_dot(high, spread) + tn_dot(mid, spread) + tn_dot(low, spread)
        for tile in range(tiles):
            coef_ref[slot, tile] = table[:, tile * LANES:(tile + 1) * LANES]

    fill(0, factors_ref[level, 1])
    fill(1, factors_ref[level, 0])
    w_high, w_low = halves(third_ref[level])
    cells = edge * edge
    for node in range(padded):
        at = slice(node * cells, (node + 1) * cells)
        if node < nodes:
            x_high, x_low = halves(block_of(node))
            start = nt_dot(x_high, w_high) + (nt_dot(x_high, w_low) + nt_dot(x_low, w_high))
        for tile in range(tiles):
            if node < nodes:
                ping_ref[tile, at, :] = start[:, tile * LANES:(tile + 1) * LANES]
            else:
                ping_ref[tile, at, :] = jnp.zeros((cells, LANES), jnp.float32)

    group = 4
    groups = edge // group

    def contract(slot, source_ref, target_ref):
        def step(index, carry):
            tile = index // groups
            first = (index % groups) * group
            sums = [jnp.zeros((rows, LANES), jnp.float32) for _ in range(group)]
            for b in range(edge):
                part = source_ref[tile, pl.ds(b, rows, stride=edge), :]
                for q in range(group):
                    factor = coef_ref[slot, tile, pl.ds((first + q) * edge + b, 1), :]
                    sums[q] = sums[q] + factor * part
            for q in range(group):
                at = pl.multiple_of((first + q) * rows, 8)
                target_ref[tile, pl.ds(at, rows), :] = sums[q]
            return carry

        lax.fori_loop(0, tiles * groups, step, 0)

    contract(0, ping_ref, pong_ref)
    contract(1, pong_ref, ping_ref)

    per_tile = LANES // edge
    columns = 2 * LANES
    lane = lax.broadcasted_iota(jnp.int32, (LANES, columns), 0)
    column = lax.broadcasted_iota(jnp.int32, (LANES, columns), 1)
    column_disp = (column // LANES) * per_tile + (column % LANES) // edge
    column_ok = (column % LANES) < per_tile * edge
    terms = pairs // disp
    total = None
    for tile in range(tiles):
        place = lane + tile * LANES
        pick = (
            (place // (edge * terms) == column_disp) & (place % edge == (column % LANES) % edge)
            & column_ok & (place < pairs * edge)
        ).astype(jnp.bfloat16)
        high, low = halves(ping_ref[tile])
        part = jnp.dot(high, pick, preferred_element_type=jnp.float32) + jnp.dot(
            low, pick, preferred_element_type=jnp.float32
        )
        total = part if total is None else total + part
    used = edge * edge * padded
    for half in range(2):
        image_ref[half, pl.ds(0, used), :] = total[:, half * LANES:(half + 1) * LANES]
        image_ref[half, pl.ds(used, image_ref.shape[1] - used), :] = jnp.zeros(
            (image_ref.shape[1] - used, LANES), jnp.float32
        )
    out_ref[...] = jnp.zeros_like(out_ref)
    out_lane = lax.broadcasted_iota(jnp.int32, (CHUNK_ROWS, LANES), 1) // edge
    for node in range(nodes):
        for e in range(disp):
            packed = jnp.zeros((CHUNK_ROWS, LANES), jnp.float32)
            for q in range(per_tile):
                chunk = image_ref[
                    e // per_tile, pl.ds(q * CHUNK_ROWS * padded + node, CHUNK_ROWS, stride=padded), :
                ]
                shift = (edge * (q - e % per_tile)) % LANES
                if shift:
                    chunk = pltpu.roll(chunk, shift, 1)
                packed = jnp.where(out_lane == q, chunk, packed)
            to = dest_ref[node, e]
            out_ref[to] = out_ref[to] + packed


def middle_images_kernel(sizes, dest_ref, x_ref, *rest):
    images_body(*sizes, lambda node: x_ref[node], 1, dest_ref, *rest)


def coarse_images_kernel(
    sizes, dest_ref, place_ref, column_ref, square_ref, lane_ref, *rest
):
    members = column_ref.shape[0]
    block = square_ref.shape[2] // 4
    spread = []
    for g in range(members):
        table = jnp.where(place_ref[0, g] % 2 == 0, lane_ref[0], lane_ref[1])
        spread.append(split_dot(tn_dot, column_ref[g], table)[:block])

    def block_of(node):
        parts = []
        for quarter in range(4):
            part = jnp.zeros((block, spread[0].shape[1]), jnp.float32)
            for g in range(members):
                here = place_ref[0, g] // 2 == node * 4 + quarter
                part = part + jnp.where(here, spread[g], 0.0)
            parts.append(part)
        return table_dot(square_ref, jnp.concatenate(parts, axis=0), spread[0].shape[1] ** 2)

    images_body(*sizes, block_of, 0, dest_ref, *rest)


VMEM = pl.BlockSpec(memory_space=pltpu.VMEM)
SMEM = pl.BlockSpec(memory_space=pltpu.SMEM)


def factor_operands(operator_blocks, ranks, edge):
    levels, disp, terms = operator_blocks.shape[:3]
    pairs = disp * terms
    width = ceil_to(pairs * edge, LANES)
    keep = (jnp.arange(terms, dtype=jnp.int32) < ranks[:, :, None]).astype(jnp.float32)
    third = (operator_blocks[:, :, :, 2] * keep[..., None]).reshape(levels, pairs * edge, edge)
    third = jnp.pad(third, ((0, 0), (0, width - pairs * edge), (0, 0)))
    factors = operator_blocks[:, :, :, :2].transpose(0, 3, 1, 2, 4)
    return third, factors.reshape(levels, 2, pairs, edge * edge)


def images(kernel, nodes, edge, disp, scalars, extra, operands, buffer_rows):
    padded = nodes + nodes % 2
    tiles = operands[0].shape[1] // LANES
    per_tile = LANES // edge
    return pl.pallas_call(
        functools.partial(kernel, (edge, disp, nodes, padded, tiles)),
        out_shape=jax.ShapeDtypeStruct((buffer_rows, CHUNK_ROWS, LANES), jnp.float32),
        in_specs=[SMEM] * len(scalars) + [VMEM] * (len(extra) + 2),
        out_specs=VMEM,
        scratch_shapes=[
            pltpu.VMEM((tiles, padded * edge * edge, LANES), jnp.float32),
            pltpu.VMEM((tiles, padded * edge * edge, LANES), jnp.float32),
            pltpu.VMEM((2, tiles, edge * edge, LANES), jnp.float32),
            pltpu.VMEM((2, padded * CHUNK_ROWS * per_tile, LANES), jnp.float32),
        ],
    )(*scalars, *extra, *operands)


def group_place(names):
    place, size = 0, 1
    for name in names:
        place = place * lax.axis_size(name) + lax.axis_index(name)
        size = size * lax.axis_size(name)
    return place, size


def group_device(names, place):
    device = {}
    for name in reversed(names):
        device[name] = lax.rem(place, lax.axis_size(name))
        place = place // lax.axis_size(name)
    return device


def greet(names):
    me, size = group_place(names)
    barrier = pltpu.get_barrier_semaphore()
    for step in range(1, size):
        pl.semaphore_signal(
            barrier, inc=1, device_id=group_device(names, lax.rem(me + step, size)),
            device_id_type=pl.DeviceIdType.MESH,
        )
    return lambda: pl.semaphore_wait(barrier, size - 1)


def group_sends(names, source_of, landed_ref, send_sem, recv_sem):
    me, size = group_place(names)
    copies = []
    for step in range(1, size):
        to = lax.rem(me + step, size)
        copies.append(
            pltpu.make_async_remote_copy(
                src_ref=source_of(to), dst_ref=landed_ref.at[me],
                send_sem=send_sem.at[step - 1], recv_sem=recv_sem.at[step - 1],
                device_id=group_device(names, to), device_id_type=pl.DeviceIdType.MESH,
            )
        )
    return copies


def forward_kernel(leaf_ref, forward_ref, h_ref, head_ref, x_ref, corner_ref):
    cells = x_ref.shape[1]
    for node in range(x_ref.shape[0]):
        rows = table_dot(forward_ref, leaf_ref[node])
        x_ref[node] = split_dot(nt_dot, rows[:cells], h_ref[...])
        corner_ref[node] = split_dot(nt_dot, head_ref[...], rows[cells:])


def corner_kernel(corner_ref, column_ref, landed_ref, send_sem, recv_sem):
    names = ("gz",)
    me, size = group_place(names)
    greet(names)()
    copies = group_sends(names, lambda to: corner_ref, landed_ref, send_sem, recv_sem)
    for copy in copies:
        copy.start()
    column_ref[pl.ds(me, 1)] = corner_ref[...][None]
    for step, copy in enumerate(copies, 1):
        copy.wait()
        source = lax.rem(me + size - step, size)
        column_ref[pl.ds(source, 1)] = landed_ref[pl.ds(source, 1)]


def unpacked(packed, edge, scratch_ref):
    for q in range(LANES // edge):
        chunk = pltpu.roll(packed, (LANES - edge * q) % LANES, 1) if q else packed
        scratch_ref[q * CHUNK_ROWS:(q + 1) * CHUNK_ROWS, :] = chunk
    return scratch_ref[...]


def back_kernel(
    place_ref, buffer_ref, inverse_ref, lane_inverse_ref, lane_back_ref, out_ref,
    scratch_ref, landed_ref, send_sem, recv_sem,
):
    names = ("gx", "gy")
    me, size = group_place(names)
    greet(names)()
    copies = group_sends(names, lambda to: buffer_ref.at[to], landed_ref, send_sem, recv_sem)
    for copy in copies:
        copy.start()
    for copy in copies:
        copy.wait()
    coarse = buffer_ref.shape[1]
    edge = out_ref.shape[2]
    block = out_ref.shape[1]
    backs = []
    for p in range(coarse):
        total = buffer_ref[me, p]
        for step in range(1, size):
            total = total + landed_ref[lax.rem(me + size - step, size), p]
        lanes = split_dot(nn_dot, unpacked(total, edge, scratch_ref), lane_inverse_ref[...])
        backs.append(table_dot(inverse_ref, lanes))
    for node in range(out_ref.shape[0]):
        place = place_ref[0, node]
        part = jnp.zeros((block, edge), jnp.float32)
        for p in range(coarse):
            for quarter in range(4):
                here = place // 2 == p * 4 + quarter
                part = part + jnp.where(here, backs[p][quarter * block:(quarter + 1) * block], 0.0)
        table = jnp.where(place % 2 == 0, lane_back_ref[0], lane_back_ref[1])
        out_ref[node] = split_dot(nn_dot, part, table)


def final_kernel(received_ref, parent_ref, inverse_ref, inner_ref, lane_inverse_ref, out_ref, scratch_ref):
    sources, nodes = received_ref.shape[:2]
    edge = out_ref.shape[2]
    for node in range(nodes):
        total = received_ref[0, node]
        for source in range(1, sources):
            total = total + received_ref[source, node]
        lanes = split_dot(nn_dot, unpacked(total, edge, scratch_ref), lane_inverse_ref[...])
        out_ref[node] = table_dot(inverse_ref, lanes) + table_dot(inner_ref, parent_ref[node])


def on_device(
    leaf_coeffs, operator_blocks, term_ranks, target_device, target_slot, coarse_targets, parent_place
):
    order = ORDER
    edge = 2 * order
    face, cells = order * order, edge * edge
    block = ceil_to(face, 8)
    table = tables(order)
    nodes = leaf_coeffs.shape[0] // 8
    coarse = coarse_targets.shape[0]
    count_gx, count_gy, count_gz = (lax.axis_size(name) for name in ("gx", "gy", "gz"))
    pad = table["head"].shape[0]
    scratch = [pltpu.VMEM((LANES // edge * CHUNK_ROWS, LANES), jnp.float32)]

    disp = operator_blocks.shape[1]
    operands = factor_operands(operator_blocks, term_ranks, edge)
    leaves = leaf_coeffs.reshape(nodes, 4, 2, face, order).transpose(0, 1, 3, 2, 4)
    leaves = jnp.pad(leaves.reshape(nodes, 4, face, edge), ((0, 0), (0, 0), (0, block - face), (0, 0)))
    middle, corners = pl.pallas_call(
        forward_kernel,
        out_shape=(
            jax.ShapeDtypeStruct((nodes, cells, edge), jnp.float32),
            jax.ShapeDtypeStruct((nodes, pad, LANES), jnp.float32),
        ),
        in_specs=[VMEM] * 4,
        out_specs=(VMEM, VMEM),
    )(leaves.reshape(nodes, 4 * block, edge), table["forward"], table["h"], table["head"])
    destination = target_device[:, :, 0] * nodes + target_slot
    middle_buffer = images(
        middle_images_kernel, nodes, edge, disp, (destination,), (middle,),
        operands, count_gy * count_gz * nodes,
    )
    middle_buffer, corners = lax.optimization_barrier((middle_buffer, corners))
    received = lax.all_to_all(middle_buffer, ("gy", "gz"), split_axis=0, concat_axis=0, tiled=True)
    column = pl.pallas_call(
        corner_kernel,
        out_shape=jax.ShapeDtypeStruct((count_gz, nodes, pad, LANES), jnp.float32),
        in_specs=[VMEM],
        out_specs=VMEM,
        scratch_shapes=[
            pltpu.VMEM((count_gz, nodes, pad, LANES), jnp.float32),
            pltpu.SemaphoreType.DMA((count_gz,)),
            pltpu.SemaphoreType.DMA((count_gz,)),
        ],
        compiler_params=pltpu.CompilerParams(collective_id=0, has_side_effects=True),
    )(corners).reshape(-1, pad, LANES)
    coarse_buffer = images(
        coarse_images_kernel, coarse, edge, disp, (coarse_targets, parent_place),
        (column, table["forward"], table["lane_place"]),
        operands, count_gx * count_gy * coarse,
    )
    own_place = lax.dynamic_slice_in_dim(parent_place, lax.axis_index("gz") * nodes, nodes, 1)
    plane = count_gx * count_gy
    parent = pl.pallas_call(
        back_kernel,
        out_shape=jax.ShapeDtypeStruct((nodes, block, edge), jnp.float32),
        in_specs=[SMEM] + [VMEM] * 4,
        out_specs=VMEM,
        scratch_shapes=scratch + [
            pltpu.VMEM((plane, coarse, CHUNK_ROWS, LANES), jnp.float32),
            pltpu.SemaphoreType.DMA((plane,)),
            pltpu.SemaphoreType.DMA((plane,)),
        ],
        compiler_params=pltpu.CompilerParams(collective_id=1, has_side_effects=True),
    )(
        own_place, coarse_buffer.reshape(plane, coarse, CHUNK_ROWS, LANES), table["inverse"],
        table["lane_inverse"], table["lane_back"],
    )
    result = pl.pallas_call(
        final_kernel,
        out_shape=jax.ShapeDtypeStruct((nodes, 4 * block, edge), jnp.float32),
        in_specs=[VMEM] * 5,
        out_specs=VMEM,
        scratch_shapes=scratch,
    )(
        received.reshape(-1, nodes, CHUNK_ROWS, LANES), parent, table["inverse"], table["inner"],
        table["lane_inverse"],
    )
    result = result.reshape(nodes, 4, block, 2, order)[:, :, :face]
    return result.transpose(0, 1, 3, 2, 4).reshape(nodes * 8, face * order)


def solution(mesh):
    in_specs = (
        P(("gx", "gy", "gz"), None),
        P(),
        P(),
        P(("gx", "gy", "gz"), None, None),
        P(("gx", "gy", "gz"), None),
        P(("gx", "gy"), None),
        P(("gx", "gy"), None),
    )
    out_specs = P(("gx", "gy", "gz"), None)
    return jax.shard_map(
        on_device, mesh=mesh, in_specs=in_specs, out_specs=out_specs, check_vma=False
    )
```

```python
import functools

import jax
import jax.numpy as jnp
import numpy as np
from jax import lax
from jax.experimental import pallas as pl
from jax.experimental.pallas import tpu as pltpu
from jax.sharding import PartitionSpec as P


ORDER = 10
LANES = 128
CHUNK_ROWS = 72


def ceil_to(value, step):
    return -(-value // step) * step


@functools.cache
def tables(order):
    edge = 2 * order
    i, x = np.arange(edge)[:, None], np.arange(edge)[None, :]
    h = np.sqrt(2.0 / edge) * np.cos(np.pi * (x + 0.5) * i / edge) * np.where(i == 0, np.sqrt(0.5), 1.0)
    face = order * order
    block = ceil_to(face, 8)
    cells = edge * edge
    per_tile = LANES // edge
    square = np.zeros((cells, 4, block))
    whole = np.einsum("ixa,jyb->ijxyab", h.reshape(edge, 2, order), h.reshape(edge, 2, order))
    square[:, :, :face] = whole.reshape(cells, 4, face)
    square = square.reshape(cells, 4 * block)
    low = square.reshape(edge, edge, -1)[:order, :order].reshape(face, -1)
    corner = np.zeros((LANES, 4 * block))
    corner[:face] = low
    forward = np.concatenate([square, corner])
    inverse = np.zeros((4 * block, per_tile * CHUNK_ROWS))
    inverse[:, :cells] = square.T
    inner = np.zeros((4 * block, block))
    inner[:, :face] = low.T
    pad = ceil_to(order, 8)
    lane_place = np.zeros((2, pad, edge))
    lane_back = np.zeros((2, edge, edge))
    for o in range(2):
        lane_place[o, :order] = h.T[o * order:(o + 1) * order]
        lane_back[o, o * order:(o + 1) * order] = h[:order]
    lane_inverse = np.zeros((LANES, edge))
    lane_inverse[:edge] = h
    head = np.zeros((pad, edge))
    head[:] = h[:pad]

    def split(value):
        high = value.astype(np.float32).astype(jnp.bfloat16)
        return np.stack([high, (value - high.astype(np.float64)).astype(np.float32).astype(jnp.bfloat16)])

    plain = lambda value: value.astype(np.float32)
    return dict(
        forward=split(forward), inverse=split(inverse), inner=split(inner),
        h=plain(h), head=plain(head), lane_place=plain(lane_place), lane_back=plain(lane_back),
        lane_inverse=plain(lane_inverse),
    )


def table_dot(table_ref, value, rows=None):
    high, low = halves(value)
    dot = lambda a, b: jnp.dot(a, b, preferred_element_type=jnp.float32)
    first, second = table_ref[0, :rows], table_ref[1, :rows]
    return dot(first, high) + (dot(first, low) + dot(second, high))


def split_dot(dot, a, b):
    a_high, a_low = halves(a)
    b_high, b_low = halves(b)
    return dot(a_high, b_high) + (dot(a_high, b_low) + dot(a_low, b_high))


def nn_dot(a, b):
    return jnp.dot(a, b, preferred_element_type=jnp.float32)


def halves(value):
    high = value.astype(jnp.bfloat16)
    low = (value - high.astype(jnp.float32)).astype(jnp.bfloat16)
    return high, low


def nt_dot(a, b):
    return lax.dot_general(a, b, (((1,), (1,)), ((), ())), preferred_element_type=jnp.float32)


def tn_dot(a, b):
    return lax.dot_general(a, b, (((0,), (0,)), ((), ())), preferred_element_type=jnp.float32)


def images_body(
    edge, disp, nodes, padded, tiles, block_of,
    level, dest_ref, third_ref, factors_ref, out_ref,
    ping_ref, pong_ref, coef_ref, image_ref,
):
    pairs = factors_ref.shape[2]
    width = tiles * LANES
    rows = padded * edge
    spread = (
        lax.broadcasted_iota(jnp.int32, (pairs, width), 1) // edge
        == lax.broadcasted_iota(jnp.int32, (pairs, width), 0)
    ).astype(jnp.bfloat16)

    def fill(slot, value):
        high = value.astype(jnp.bfloat16)
        rest = value - high.astype(jnp.float32)
        mid, low = halves(rest)
        table = tn_dot(high, spread) + tn_dot(mid, spread) + tn_dot(low, spread)
        for tile in range(tiles):
            coef_ref[slot, tile] = table[:, tile * LANES:(tile + 1) * LANES]

    fill(0, factors_ref[level, 1])
    fill(1, factors_ref[level, 0])
    w_high, w_low = halves(third_ref[level])
    cells = edge * edge
    for node in range(padded):
        at = slice(node * cells, (node + 1) * cells)
        if node < nodes:
            x_high, x_low = halves(block_of(node))
            start = nt_dot(x_high, w_high) + (nt_dot(x_high, w_low) + nt_dot(x_low, w_high))
        for tile in range(tiles):
            if node < nodes:
                ping_ref[tile, at, :] = start[:, tile * LANES:(tile + 1) * LANES]
            else:
                ping_ref[tile, at, :] = jnp.zeros((cells, LANES), jnp.float32)

    group = 4
    groups = edge // group

    def contract(slot, source_ref, target_ref):
        def step(index, carry):
            tile = index // groups
            first = (index % groups) * group
            sums = [jnp.zeros((rows, LANES), jnp.float32) for _ in range(group)]
            for b in range(edge):
                part = source_ref[tile, pl.ds(b, rows, stride=edge), :]
                for q in range(group):
                    factor = coef_ref[slot, tile, pl.ds((first + q) * edge + b, 1), :]
                    sums[q] = sums[q] + factor * part
            for q in range(group):
                at = pl.multiple_of((first + q) * rows, 8)
                target_ref[tile, pl.ds(at, rows), :] = sums[q]
            return carry

        lax.fori_loop(0, tiles * groups, step, 0)

    contract(0, ping_ref, pong_ref)
    contract(1, pong_ref, ping_ref)

    per_tile = LANES // edge
    columns = 2 * LANES
    lane = lax.broadcasted_iota(jnp.int32, (LANES, columns), 0)
    column = lax.broadcasted_iota(jnp.int32, (LANES, columns), 1)
    column_disp = (column // LANES) * per_tile + (column % LANES) // edge
    column_ok = (column % LANES) < per_tile * edge
    terms = pairs // disp
    total = None
    for tile in range(tiles):
        place = lane + tile * LANES
        pick = (
            (place // (edge * terms) == column_disp) & (place % edge == (column % LANES) % edge)
            & column_ok & (place < pairs * edge)
        ).astype(jnp.bfloat16)
        high, low = halves(ping_ref[tile])
        part = jnp.dot(high, pick, preferred_element_type=jnp.float32) + jnp.dot(
            low, pick, preferred_element_type=jnp.float32
        )
        total = part if total is None else total + part
    used = edge * edge * padded
    for half in range(2):
        image_ref[half, pl.ds(0, used), :] = total[:, half * LANES:(half + 1) * LANES]
        image_ref[half, pl.ds(used, image_ref.shape[1] - used), :] = jnp.zeros(
            (image_ref.shape[1] - used, LANES), jnp.float32
        )
    out_ref[...] = jnp.zeros_like(out_ref)
    out_lane = lax.broadcasted_iota(jnp.int32, (CHUNK_ROWS, LANES), 1) // edge
    for node in range(nodes):
        for e in range(disp):
            packed = jnp.zeros((CHUNK_ROWS, LANES), jnp.float32)
            for q in range(per_tile):
                chunk = image_ref[
                    e // per_tile, pl.ds(q * CHUNK_ROWS * padded + node, CHUNK_ROWS, stride=padded), :
                ]
                shift = (edge * (q - e % per_tile)) % LANES
                if shift:
                    chunk = pltpu.roll(chunk, shift, 1)
                packed = jnp.where(out_lane == q, chunk, packed)
            to = dest_ref[node, e]
            out_ref[to] = out_ref[to] + packed


def middle_images_kernel(sizes, dest_ref, x_ref, *rest):
    images_body(*sizes, lambda node: x_ref[node], 1, dest_ref, *rest)


def coarse_images_kernel(
    sizes, dest_ref, place_ref, column_ref, square_ref, lane_ref, *rest
):
    members = column_ref.shape[0]
    block = square_ref.shape[2] // 4
    spread = []
    for g in range(members):
        table = jnp.where(place_ref[0, g] % 2 == 0, lane_ref[0], lane_ref[1])
        spread.append(split_dot(tn_dot, column_ref[g], table)[:block])

    def block_of(node):
        parts = []
        for quarter in range(4):
            part = jnp.zeros((block, spread[0].shape[1]), jnp.float32)
            for g in range(members):
                here = place_ref[0, g] // 2 == node * 4 + quarter
                part = part + jnp.where(here, spread[g], 0.0)
            parts.append(part)
        return table_dot(square_ref, jnp.concatenate(parts, axis=0), spread[0].shape[1] ** 2)

    images_body(*sizes, block_of, 0, dest_ref, *rest)


VMEM = pl.BlockSpec(memory_space=pltpu.VMEM)
SMEM = pl.BlockSpec(memory_space=pltpu.SMEM)


def factor_operands(operator_blocks, ranks, edge):
    levels, disp, terms = operator_blocks.shape[:3]
    pairs = disp * terms
    width = ceil_to(pairs * edge, LANES)
    keep = (jnp.arange(terms, dtype=jnp.int32) < ranks[:, :, None]).astype(jnp.float32)
    third = (operator_blocks[:, :, :, 2] * keep[..., None]).reshape(levels, pairs * edge, edge)
    third = jnp.pad(third, ((0, 0), (0, width - pairs * edge), (0, 0)))
    factors = operator_blocks[:, :, :, :2].transpose(0, 3, 1, 2, 4)
    return third, factors.reshape(levels, 2, pairs, edge * edge)


def images(kernel, nodes, edge, disp, scalars, extra, operands, buffer_rows):
    padded = nodes + nodes % 2
    tiles = operands[0].shape[1] // LANES
    per_tile = LANES // edge
    return pl.pallas_call(
        functools.partial(kernel, (edge, disp, nodes, padded, tiles)),
        out_shape=jax.ShapeDtypeStruct((buffer_rows, CHUNK_ROWS, LANES), jnp.float32),
        in_specs=[SMEM] * len(scalars) + [VMEM] * (len(extra) + 2),
        out_specs=VMEM,
        scratch_shapes=[
            pltpu.VMEM((tiles, padded * edge * edge, LANES), jnp.float32),
            pltpu.VMEM((tiles, padded * edge * edge, LANES), jnp.float32),
            pltpu.VMEM((2, tiles, edge * edge, LANES), jnp.float32),
            pltpu.VMEM((2, padded * CHUNK_ROWS * per_tile, LANES), jnp.float32),
        ],
    )(*scalars, *extra, *operands)


def group_place(names):
    place, size = 0, 1
    for name in names:
        place = place * lax.axis_size(name) + lax.axis_index(name)
        size = size * lax.axis_size(name)
    return place, size


def group_device(names, place):
    device = {}
    for name in reversed(names):
        device[name] = lax.rem(place, lax.axis_size(name))
        place = place // lax.axis_size(name)
    return device


def greet(names):
    me, size = group_place(names)
    barrier = pltpu.get_barrier_semaphore()
    for step in range(1, size):
        pl.semaphore_signal(
            barrier, inc=1, device_id=group_device(names, lax.rem(me + step, size)),
            device_id_type=pl.DeviceIdType.MESH,
        )
    return lambda: pl.semaphore_wait(barrier, size - 1)


def group_sends(names, source_of, landed_ref, send_sem, recv_sem):
    me, size = group_place(names)
    copies = []
    for step in range(1, size):
        to = lax.rem(me + step, size)
        copies.append(
            pltpu.make_async_remote_copy(
                src_ref=source_of(to), dst_ref=landed_ref.at[me],
                send_sem=send_sem.at[step - 1], recv_sem=recv_sem.at[step - 1],
                device_id=group_device(names, to), device_id_type=pl.DeviceIdType.MESH,
            )
        )
    return copies


def forward_kernel(
    leaf_ref, forward_ref, h_ref, head_ref, x_ref, column_ref, corner_ref, landed_ref, send_sem, recv_sem
):
    names = ("gz",)
    me, size = group_place(names)
    greeted = greet(names)
    cells = x_ref.shape[1]
    nodes = x_ref.shape[0]
    for node in range(nodes):
        rows = table_dot(forward_ref, leaf_ref[node])
        x_ref[node] = split_dot(nt_dot, rows[:cells], h_ref[...])
        corner_ref[node] = split_dot(nt_dot, head_ref[...], rows[cells:])
    greeted()
    copies = group_sends(names, lambda to: corner_ref, landed_ref, send_sem, recv_sem)
    for copy in copies:
        copy.start()
    column_ref[pl.ds(me, 1)] = corner_ref[...][None]
    for step, copy in enumerate(copies, 1):
        copy.wait()
        source = lax.rem(me + size - step, size)
        column_ref[pl.ds(source, 1)] = landed_ref[pl.ds(source, 1)]


def unpacked(packed, edge, scratch_ref):
    for q in range(LANES // edge):
        chunk = pltpu.roll(packed, (LANES - edge * q) % LANES, 1) if q else packed
        scratch_ref[q * CHUNK_ROWS:(q + 1) * CHUNK_ROWS, :] = chunk
    return scratch_ref[...]


def back_kernel(
    place_ref, buffer_ref, inverse_ref, lane_inverse_ref, lane_back_ref, out_ref,
    scratch_ref, landed_ref, send_sem, recv_sem,
):
    names = ("gx", "gy")
    me, size = group_place(names)
    greet(names)()
    copies = group_sends(names, lambda to: buffer_ref.at[to], landed_ref, send_sem, recv_sem)
    for copy in copies:
        copy.start()
    for copy in copies:
        copy.wait()
    coarse = buffer_ref.shape[1]
    edge = out_ref.shape[2]
    block = out_ref.shape[1]
    backs = []
    for p in range(coarse):
        total = buffer_ref[me, p]
        for step in range(1, size):
            total = total + landed_ref[lax.rem(me + size - step, size), p]
        lanes = split_dot(nn_dot, unpacked(total, edge, scratch_ref), lane_inverse_ref[...])
        backs.append(table_dot(inverse_ref, lanes))
    for node in range(out_ref.shape[0]):
        place = place_ref[0, node]
        part = jnp.zeros((block, edge), jnp.float32)
        for p in range(coarse):
            for quarter in range(4):
                here = place // 2 == p * 4 + quarter
                part = part + jnp.where(here, backs[p][quarter * block:(quarter + 1) * block], 0.0)
        table = jnp.where(place % 2 == 0, lane_back_ref[0], lane_back_ref[1])
        out_ref[node] = split_dot(nn_dot, part, table)


def final_kernel(received_ref, parent_ref, inverse_ref, inner_ref, lane_inverse_ref, out_ref, scratch_ref):
    sources, nodes = received_ref.shape[:2]
    edge = out_ref.shape[2]
    for node in range(nodes):
        total = received_ref[0, node]
        for source in range(1, sources):
            total = total + received_ref[source, node]
        lanes = split_dot(nn_dot, unpacked(total, edge, scratch_ref), lane_inverse_ref[...])
        out_ref[node] = table_dot(inverse_ref, lanes) + table_dot(inner_ref, parent_ref[node])


def on_device(
    leaf_coeffs, operator_blocks, term_ranks, target_device, target_slot, coarse_targets, parent_place
):
    order = ORDER
    edge = 2 * order
    face, cells = order * order, edge * edge
    block = ceil_to(face, 8)
    table = tables(order)
    nodes = leaf_coeffs.shape[0] // 8
    coarse = coarse_targets.shape[0]
    count_gx, count_gy, count_gz = (lax.axis_size(name) for name in ("gx", "gy", "gz"))
    pad = table["head"].shape[0]
    scratch = [pltpu.VMEM((LANES // edge * CHUNK_ROWS, LANES), jnp.float32)]

    disp = operator_blocks.shape[1]
    operands = factor_operands(operator_blocks, term_ranks, edge)
    leaves = leaf_coeffs.reshape(nodes, 4, 2, face, order).transpose(0, 1, 3, 2, 4)
    leaves = jnp.pad(leaves.reshape(nodes, 4, face, edge), ((0, 0), (0, 0), (0, block - face), (0, 0)))
    middle, column = pl.pallas_call(
        forward_kernel,
        out_shape=(
            jax.ShapeDtypeStruct((nodes, cells, edge), jnp.float32),
            jax.ShapeDtypeStruct((count_gz, nodes, pad, LANES), jnp.float32),
        ),
        in_specs=[VMEM] * 4,
        out_specs=(VMEM, VMEM),
        scratch_shapes=[
            pltpu.VMEM((nodes, pad, LANES), jnp.float32),
            pltpu.VMEM((count_gz, nodes, pad, LANES), jnp.float32),
            pltpu.SemaphoreType.DMA((count_gz,)),
            pltpu.SemaphoreType.DMA((count_gz,)),
        ],
        compiler_params=pltpu.CompilerParams(collective_id=0, has_side_effects=True),
    )(leaves.reshape(nodes, 4 * block, edge), table["forward"], table["h"], table["head"])
    column = column.reshape(-1, pad, LANES)
    destination = target_device[:, :, 0] * nodes + target_slot
    middle_buffer = images(
        middle_images_kernel, nodes, edge, disp, (destination,), (middle,),
        operands, count_gy * count_gz * nodes,
    )
    middle_buffer, column = lax.optimization_barrier((middle_buffer, column))
    received = lax.all_to_all(middle_buffer, ("gy", "gz"), split_axis=0, concat_axis=0, tiled=True)
    coarse_buffer = images(
        coarse_images_kernel, coarse, edge, disp, (coarse_targets, parent_place),
        (column, table["forward"], table["lane_place"]),
        operands, count_gx * count_gy * coarse,
    )
    own_place = lax.dynamic_slice_in_dim(parent_place, lax.axis_index("gz") * nodes, nodes, 1)
    plane = count_gx * count_gy
    parent = pl.pallas_call(
        back_kernel,
        out_shape=jax.ShapeDtypeStruct((nodes, block, edge), jnp.float32),
        in_specs=[SMEM] + [VMEM] * 4,
        out_specs=VMEM,
        scratch_shapes=scratch + [
            pltpu.VMEM((plane, coarse, CHUNK_ROWS, LANES), jnp.float32),
            pltpu.SemaphoreType.DMA((plane,)),
            pltpu.SemaphoreType.DMA((plane,)),
        ],
        compiler_params=pltpu.CompilerParams(collective_id=1, has_side_effects=True),
    )(
        own_place, coarse_buffer.reshape(plane, coarse, CHUNK_ROWS, LANES), table["inverse"],
        table["lane_inverse"], table["lane_back"],
    )
    result = pl.pallas_call(
        final_kernel,
        out_shape=jax.ShapeDtypeStruct((nodes, 4 * block, edge), jnp.float32),
        in_specs=[VMEM] * 5,
        out_specs=VMEM,
        scratch_shapes=scratch,
    )(
        received.reshape(-1, nodes, CHUNK_ROWS, LANES), parent, table["inverse"], table["inner"],
        table["lane_inverse"],
    )
    result = result.reshape(nodes, 4, block, 2, order)[:, :, :face]
    return result.transpose(0, 1, 3, 2, 4).reshape(nodes * 8, face * order)


def solution(mesh):
    in_specs = (
        P(("gx", "gy", "gz"), None),
        P(),
        P(),
        P(("gx", "gy", "gz"), None, None),
        P(("gx", "gy", "gz"), None),
        P(("gx", "gy"), None),
        P(("gx", "gy"), None),
    )
    out_specs = P(("gx", "gy", "gz"), None)
    return jax.shard_map(
        on_device, mesh=mesh, in_specs=in_specs, out_specs=out_specs, check_vma=False
    )
```

```python
import functools

import jax
import jax.numpy as jnp
import numpy as np
from jax import lax
from jax.experimental import pallas as pl
from jax.experimental.pallas import tpu as pltpu
from jax.sharding import PartitionSpec as P


ORDER = 10
LANES = 128
CHUNK_ROWS = 72


def ceil_to(value, step):
    return -(-value // step) * step


@functools.cache
def tables(order):
    edge = 2 * order
    i, x = np.arange(edge)[:, None], np.arange(edge)[None, :]
    h = np.sqrt(2.0 / edge) * np.cos(np.pi * (x + 0.5) * i / edge) * np.where(i == 0, np.sqrt(0.5), 1.0)
    face = order * order
    block = ceil_to(face, 8)
    cells = edge * edge
    per_tile = LANES // edge
    square = np.zeros((cells, 4, block))
    whole = np.einsum("ixa,jyb->ijxyab", h.reshape(edge, 2, order), h.reshape(edge, 2, order))
    square[:, :, :face] = whole.reshape(cells, 4, face)
    square = square.reshape(cells, 4 * block)
    low = square.reshape(edge, edge, -1)[:order, :order].reshape(face, -1)
    corner = np.zeros((LANES, 4 * block))
    corner[:face] = low
    forward = np.concatenate([square, corner])
    inverse = np.zeros((4 * block, per_tile * CHUNK_ROWS))
    inverse[:, :cells] = square.T
    inner = np.zeros((4 * block, block))
    inner[:, :face] = low.T
    pad = ceil_to(order, 8)
    lane_place = np.zeros((2, pad, edge))
    lane_back = np.zeros((2, edge, edge))
    for o in range(2):
        lane_place[o, :order] = h.T[o * order:(o + 1) * order]
        lane_back[o, o * order:(o + 1) * order] = h[:order]
    lane_inverse = np.zeros((LANES, edge))
    lane_inverse[:edge] = h
    head = np.zeros((pad, edge))
    head[:] = h[:pad]

    def split(value):
        high = value.astype(np.float32).astype(jnp.bfloat16)
        return np.stack([high, (value - high.astype(np.float64)).astype(np.float32).astype(jnp.bfloat16)])

    plain = lambda value: value.astype(np.float32)
    return dict(
        forward=split(forward), inverse=split(inverse), inner=split(inner),
        h=plain(h), head=plain(head), lane_place=plain(lane_place), lane_back=plain(lane_back),
        lane_inverse=plain(lane_inverse),
    )


def table_dot(table_ref, value, rows=None):
    high, low = halves(value)
    dot = lambda a, b: jnp.dot(a, b, preferred_element_type=jnp.float32)
    first, second = table_ref[0, :rows], table_ref[1, :rows]
    return dot(first, high) + (dot(first, low) + dot(second, high))


def split_dot(dot, a, b):
    a_high, a_low = halves(a)
    b_high, b_low = halves(b)
    return dot(a_high, b_high) + (dot(a_high, b_low) + dot(a_low, b_high))


def nn_dot(a, b):
    return jnp.dot(a, b, preferred_element_type=jnp.float32)


def halves(value):
    high = value.astype(jnp.bfloat16)
    low = (value - high.astype(jnp.float32)).astype(jnp.bfloat16)
    return high, low


def nt_dot(a, b):
    return lax.dot_general(a, b, (((1,), (1,)), ((), ())), preferred_element_type=jnp.float32)


def tn_dot(a, b):
    return lax.dot_general(a, b, (((0,), (0,)), ((), ())), preferred_element_type=jnp.float32)


def images_body(
    edge, disp, nodes, padded, tiles, block_of,
    level, dest_ref, third_ref, factors_ref, out_ref,
    ping_ref, pong_ref, coef_ref, image_ref,
):
    pairs = factors_ref.shape[2]
    width = tiles * LANES
    rows = padded * edge
    spread = (
        lax.broadcasted_iota(jnp.int32, (pairs, width), 1) // edge
        == lax.broadcasted_iota(jnp.int32, (pairs, width), 0)
    ).astype(jnp.bfloat16)

    def fill(slot, value):
        high, low = halves(value)
        table = tn_dot(high, spread) + tn_dot(low, spread)
        for tile in range(tiles):
            coef_ref[slot, tile] = table[:, tile * LANES:(tile + 1) * LANES]

    fill(0, factors_ref[level, 1])
    fill(1, factors_ref[level, 0])
    w_high, w_low = halves(third_ref[level])
    cells = edge * edge
    for node in range(padded):
        at = slice(node * cells, (node + 1) * cells)
        if node < nodes:
            x_high, x_low = halves(block_of(node))
            start = nt_dot(x_high, w_high) + (nt_dot(x_high, w_low) + nt_dot(x_low, w_high))
        for tile in range(tiles):
            if node < nodes:
                ping_ref[tile, at, :] = start[:, tile * LANES:(tile + 1) * LANES]
            else:
                ping_ref[tile, at, :] = jnp.zeros((cells, LANES), jnp.float32)

    group = 5
    groups = edge // group

    def contract(slot, source_ref, target_ref):
        def step(index, carry):
            tile = index // groups
            first = (index % groups) * group
            sums = [jnp.zeros((rows, LANES), jnp.float32) for _ in range(group)]
            for b in range(edge):
                part = source_ref[tile, pl.ds(b, rows, stride=edge), :]
                for q in range(group):
                    factor = coef_ref[slot, tile, pl.ds((first + q) * edge + b, 1), :]
                    sums[q] = sums[q] + factor * part
            for q in range(group):
                at = pl.multiple_of((first + q) * rows, 8)
                target_ref[tile, pl.ds(at, rows), :] = sums[q]
            return carry

        lax.fori_loop(0, tiles * groups, step, 0)

    contract(0, ping_ref, pong_ref)
    contract(1, pong_ref, ping_ref)

    per_tile = LANES // edge
    columns = 2 * LANES
    lane = lax.broadcasted_iota(jnp.int32, (LANES, columns), 0)
    column = lax.broadcasted_iota(jnp.int32, (LANES, columns), 1)
    column_disp = (column // LANES) * per_tile + (column % LANES) // edge
    column_ok = (column % LANES) < per_tile * edge
    terms = pairs // disp
    total = None
    for tile in range(tiles):
        place = lane + tile * LANES
        pick = (
            (place // (edge * terms) == column_disp) & (place % edge == (column % LANES) % edge)
            & column_ok & (place < pairs * edge)
        ).astype(jnp.bfloat16)
        high, low = halves(ping_ref[tile])
        part = jnp.dot(high, pick, preferred_element_type=jnp.float32) + jnp.dot(
            low, pick, preferred_element_type=jnp.float32
        )
        total = part if total is None else total + part
    used = edge * edge * padded
    for half in range(2):
        image_ref[half, pl.ds(0, used), :] = total[:, half * LANES:(half + 1) * LANES]
        image_ref[half, pl.ds(used, image_ref.shape[1] - used), :] = jnp.zeros(
            (image_ref.shape[1] - used, LANES), jnp.float32
        )
    out_ref[...] = jnp.zeros_like(out_ref)
    out_lane = lax.broadcasted_iota(jnp.int32, (CHUNK_ROWS, LANES), 1) // edge
    for node in range(nodes):
        for e in range(disp):
            packed = jnp.zeros((CHUNK_ROWS, LANES), jnp.float32)
            for q in range(per_tile):
                chunk = image_ref[
                    e // per_tile, pl.ds(q * CHUNK_ROWS * padded + node, CHUNK_ROWS, stride=padded), :
                ]
                shift = (edge * (q - e % per_tile)) % LANES
                if shift:
                    chunk = pltpu.roll(chunk, shift, 1)
                packed = jnp.where(out_lane == q, chunk, packed)
            to = dest_ref[node, e]
            out_ref[to] = out_ref[to] + packed


def middle_images_kernel(sizes, dest_ref, x_ref, *rest):
    images_body(*sizes, lambda node: x_ref[node], 1, dest_ref, *rest)


def coarse_images_kernel(
    sizes, dest_ref, place_ref, column_ref, square_ref, lane_ref, *rest
):
    members = column_ref.shape[0]
    block = square_ref.shape[2] // 4
    spread = []
    for g in range(members):
        table = jnp.where(place_ref[0, g] % 2 == 0, lane_ref[0], lane_ref[1])
        spread.append(split_dot(tn_dot, column_ref[g], table)[:block])

    def block_of(node):
        parts = []
        for quarter in range(4):
            part = jnp.zeros((block, spread[0].shape[1]), jnp.float32)
            for g in range(members):
                here = place_ref[0, g] // 2 == node * 4 + quarter
                part = part + jnp.where(here, spread[g], 0.0)
            parts.append(part)
        return table_dot(square_ref, jnp.concatenate(parts, axis=0), spread[0].shape[1] ** 2)

    images_body(*sizes, block_of, 0, dest_ref, *rest)


VMEM = pl.BlockSpec(memory_space=pltpu.VMEM)
SMEM = pl.BlockSpec(memory_space=pltpu.SMEM)


def factor_operands(operator_blocks, ranks, edge):
    levels, disp, terms = operator_blocks.shape[:3]
    pairs = disp * terms
    width = ceil_to(pairs * edge, LANES)
    keep = (jnp.arange(terms, dtype=jnp.int32) < ranks[:, :, None]).astype(jnp.float32)
    third = (operator_blocks[:, :, :, 2] * keep[..., None]).reshape(levels, pairs * edge, edge)
    third = jnp.pad(third, ((0, 0), (0, width - pairs * edge), (0, 0)))
    factors = operator_blocks[:, :, :, :2].transpose(0, 3, 1, 2, 4)
    return third, factors.reshape(levels, 2, pairs, edge * edge)


def images(kernel, nodes, edge, disp, scalars, extra, operands, buffer_rows):
    padded = nodes + nodes % 2
    tiles = operands[0].shape[1] // LANES
    per_tile = LANES // edge
    return pl.pallas_call(
        functools.partial(kernel, (edge, disp, nodes, padded, tiles)),
        out_shape=jax.ShapeDtypeStruct((buffer_rows, CHUNK_ROWS, LANES), jnp.float32),
        in_specs=[SMEM] * len(scalars) + [VMEM] * (len(extra) + 2),
        out_specs=VMEM,
        scratch_shapes=[
            pltpu.VMEM((tiles, padded * edge * edge, LANES), jnp.float32),
            pltpu.VMEM((tiles, padded * edge * edge, LANES), jnp.float32),
            pltpu.VMEM((2, tiles, edge * edge, LANES), jnp.float32),
            pltpu.VMEM((2, padded * CHUNK_ROWS * per_tile, LANES), jnp.float32),
        ],
    )(*scalars, *extra, *operands)


def group_place(names):
    place, size = 0, 1
    for name in names:
        place = place * lax.axis_size(name) + lax.axis_index(name)
        size = size * lax.axis_size(name)
    return place, size


def group_device(names, place):
    device = {}
    for name in reversed(names):
        device[name] = lax.rem(place, lax.axis_size(name))
        place = place // lax.axis_size(name)
    return device


def greet(names):
    me, size = group_place(names)
    barrier = pltpu.get_barrier_semaphore()
    for step in range(1, size):
        pl.semaphore_signal(
            barrier, inc=1, device_id=group_device(names, lax.rem(me + step, size)),
            device_id_type=pl.DeviceIdType.MESH,
        )
    return lambda: pl.semaphore_wait(barrier, size - 1)


def group_sends(names, source_of, landed_ref, send_sem, recv_sem):
    me, size = group_place(names)
    copies = []
    for step in range(1, size):
        to = lax.rem(me + step, size)
        copies.append(
            pltpu.make_async_remote_copy(
                src_ref=source_of(to), dst_ref=landed_ref.at[me],
                send_sem=send_sem.at[step - 1], recv_sem=recv_sem.at[step - 1],
                device_id=group_device(names, to), device_id_type=pl.DeviceIdType.MESH,
            )
        )
    return copies


def forward_kernel(
    leaf_ref, forward_ref, h_ref, head_ref, x_ref, column_ref, corner_ref, landed_ref, send_sem, recv_sem
):
    names = ("gz",)
    me, size = group_place(names)
    greeted = greet(names)
    cells = x_ref.shape[1]
    nodes = x_ref.shape[0]
    for node in range(nodes):
        rows = table_dot(forward_ref, leaf_ref[node])
        x_ref[node] = split_dot(nt_dot, rows[:cells], h_ref[...])
        corner_ref[node] = split_dot(nt_dot, head_ref[...], rows[cells:])
    greeted()
    copies = group_sends(names, lambda to: corner_ref, landed_ref, send_sem, recv_sem)
    for copy in copies:
        copy.start()
    column_ref[pl.ds(me, 1)] = corner_ref[...][None]
    for step, copy in enumerate(copies, 1):
        copy.wait()
        source = lax.rem(me + size - step, size)
        column_ref[pl.ds(source, 1)] = landed_ref[pl.ds(source, 1)]


def unpacked(packed, edge, scratch_ref):
    for q in range(LANES // edge):
        chunk = pltpu.roll(packed, (LANES - edge * q) % LANES, 1) if q else packed
        scratch_ref[q * CHUNK_ROWS:(q + 1) * CHUNK_ROWS, :] = chunk
    return scratch_ref[...]


def back_kernel(
    place_ref, buffer_ref, inverse_ref, lane_inverse_ref, lane_back_ref, out_ref,
    scratch_ref, landed_ref, send_sem, recv_sem,
):
    names = ("gx", "gy")
    me, size = group_place(names)
    greet(names)()
    copies = group_sends(names, lambda to: buffer_ref.at[to], landed_ref, send_sem, recv_sem)
    for copy in copies:
        copy.start()
    for copy in copies:
        copy.wait()
    coarse = buffer_ref.shape[1]
    edge = out_ref.shape[2]
    block = out_ref.shape[1]
    backs = []
    for p in range(coarse):
        total = buffer_ref[me, p]
        for step in range(1, size):
            total = total + landed_ref[lax.rem(me + size - step, size), p]
        lanes = split_dot(nn_dot, unpacked(total, edge, scratch_ref), lane_inverse_ref[...])
        backs.append(table_dot(inverse_ref, lanes))
    for node in range(out_ref.shape[0]):
        place = place_ref[0, node]
        part = jnp.zeros((block, edge), jnp.float32)
        for p in range(coarse):
            for quarter in range(4):
                here = place // 2 == p * 4 + quarter
                part = part + jnp.where(here, backs[p][quarter * block:(quarter + 1) * block], 0.0)
        table = jnp.where(place % 2 == 0, lane_back_ref[0], lane_back_ref[1])
        out_ref[node] = split_dot(nn_dot, part, table)


def final_kernel(received_ref, parent_ref, inverse_ref, inner_ref, lane_inverse_ref, out_ref, scratch_ref):
    sources, nodes = received_ref.shape[:2]
    edge = out_ref.shape[2]
    for node in range(nodes):
        total = received_ref[0, node]
        for source in range(1, sources):
            total = total + received_ref[source, node]
        lanes = split_dot(nn_dot, unpacked(total, edge, scratch_ref), lane_inverse_ref[...])
        out_ref[node] = table_dot(inverse_ref, lanes) + table_dot(inner_ref, parent_ref[node])


def on_device(
    leaf_coeffs, operator_blocks, term_ranks, target_device, target_slot, coarse_targets, parent_place
):
    order = ORDER
    edge = 2 * order
    face, cells = order * order, edge * edge
    block = ceil_to(face, 8)
    table = tables(order)
    nodes = leaf_coeffs.shape[0] // 8
    coarse = coarse_targets.shape[0]
    count_gx, count_gy, count_gz = (lax.axis_size(name) for name in ("gx", "gy", "gz"))
    pad = table["head"].shape[0]
    scratch = [pltpu.VMEM((LANES // edge * CHUNK_ROWS, LANES), jnp.float32)]

    disp = operator_blocks.shape[1]
    operands = factor_operands(operator_blocks, term_ranks, edge)
    leaves = leaf_coeffs.reshape(nodes, 4, 2, face, order).transpose(0, 1, 3, 2, 4)
    leaves = jnp.pad(leaves.reshape(nodes, 4, face, edge), ((0, 0), (0, 0), (0, block - face), (0, 0)))
    middle, column = pl.pallas_call(
        forward_kernel,
        out_shape=(
            jax.ShapeDtypeStruct((nodes, cells, edge), jnp.float32),
            jax.ShapeDtypeStruct((count_gz, nodes, pad, LANES), jnp.float32),
        ),
        in_specs=[VMEM] * 4,
        out_specs=(VMEM, VMEM),
        scratch_shapes=[
            pltpu.VMEM((nodes, pad, LANES), jnp.float32),
            pltpu.VMEM((count_gz, nodes, pad, LANES), jnp.float32),
            pltpu.SemaphoreType.DMA((count_gz,)),
            pltpu.SemaphoreType.DMA((count_gz,)),
        ],
        compiler_params=pltpu.CompilerParams(collective_id=0, has_side_effects=True),
    )(leaves.reshape(nodes, 4 * block, edge), table["forward"], table["h"], table["head"])
    column = column.reshape(-1, pad, LANES)
    destination = target_device[:, :, 0] * nodes + target_slot
    middle_buffer = images(
        middle_images_kernel, nodes, edge, disp, (destination,), (middle,),
        operands, count_gy * count_gz * nodes,
    )
    middle_buffer, column = lax.optimization_barrier((middle_buffer, column))
    received = lax.all_to_all(middle_buffer, ("gy", "gz"), split_axis=0, concat_axis=0, tiled=True)
    coarse_buffer = images(
        coarse_images_kernel, coarse, edge, disp, (coarse_targets, parent_place),
        (column, table["forward"], table["lane_place"]),
        operands, count_gx * count_gy * coarse,
    )
    own_place = lax.dynamic_slice_in_dim(parent_place, lax.axis_index("gz") * nodes, nodes, 1)
    plane = count_gx * count_gy
    parent = pl.pallas_call(
        back_kernel,
        out_shape=jax.ShapeDtypeStruct((nodes, block, edge), jnp.float32),
        in_specs=[SMEM] + [VMEM] * 4,
        out_specs=VMEM,
        scratch_shapes=scratch + [
            pltpu.VMEM((plane, coarse, CHUNK_ROWS, LANES), jnp.float32),
            pltpu.SemaphoreType.DMA((plane,)),
            pltpu.SemaphoreType.DMA((plane,)),
        ],
        compiler_params=pltpu.CompilerParams(collective_id=1, has_side_effects=True),
    )(
        own_place, coarse_buffer.reshape(plane, coarse, CHUNK_ROWS, LANES), table["inverse"],
        table["lane_inverse"], table["lane_back"],
    )
    result = pl.pallas_call(
        final_kernel,
        out_shape=jax.ShapeDtypeStruct((nodes, 4 * block, edge), jnp.float32),
        in_specs=[VMEM] * 5,
        out_specs=VMEM,
        scratch_shapes=scratch,
    )(
        received.reshape(-1, nodes, CHUNK_ROWS, LANES), parent, table["inverse"], table["inner"],
        table["lane_inverse"],
    )
    result = result.reshape(nodes, 4, block, 2, order)[:, :, :face]
    return result.transpose(0, 1, 3, 2, 4).reshape(nodes * 8, face * order)


def solution(mesh):
    in_specs = (
        P(("gx", "gy", "gz"), None),
        P(),
        P(),
        P(("gx", "gy", "gz"), None, None),
        P(("gx", "gy", "gz"), None),
        P(("gx", "gy"), None),
        P(("gx", "gy"), None),
    )
    out_specs = P(("gx", "gy", "gz"), None)
    return jax.shard_map(
        on_device, mesh=mesh, in_specs=in_specs, out_specs=out_specs, check_vma=False
    )
```
